32 devices in a mesh: groups: 2 (over y), seq: 4 (over z), tensor: 4 (over x, core).
Axes of the slice: x: 2, y: 2, z: 4, core: 2. Of those that a mesh axis runs over, the one named last changes fastest.
Arguments:
- residual_in: float32 [1024, 4096], P(('groups', 'seq'), 'tensor'), parts along dimension 0, may hold values from -48 to 48
- norm_gain: float32 [4096], replicated, may hold values from 0.1 to 1.9
- in_weight: bfloat16 [3, 4096, 2048], P(None, 'seq', 'tensor'), may hold values from -0.09375 to 0.09375
- short_taps: float32 [3, 3, 2048], P(None, None, 'tensor'), may hold values from -3 to 3
- long_filter: float32 [2048, 512], P(('tensor', 'seq')), may hold values from -0.25 to 0.25
- out_weight: bfloat16 [4096, 2048], P('seq', 'tensor'), may hold values from -0.125 to 0.125
Outputs:
- block_out: float32 [1024, 4096], P(('groups', 'seq'), 'tensor'), parts along dimension 0
The draws below stay inside these ranges and needn't reach their ends.
There are 2 independent parts, one for each index of `groups`. The reference program is written for one: setup_inputs(seed, part) draws one part's arguments, and reference() takes and returns one part's arrays. A program takes and returns all parts, laid end to end along the dimension named above; an argument that names none is the same for every part. Nothing has to cross between parts.
All inputs are finite; a program needn't handle non-finite values.
Results may differ from the reference program's by a relative error of at most 0.015.
Values may be sent and summed in bfloat16 or wider, within the bound.
No kernel may reach another device: no remote copies, remote signals or barrier semaphores. Data moves between devices by JAX's collectives and lax.ppermute only.
A program may use at most 64 MiB of HBM per device.

```python
import math
import jax
import jax.numpy as jnp
from jax import lax

D = 4096
CH = 2048
TAPS = 3
L = 512
N_TENSOR = 4


def draw_residual_in(key, part):
    first, second, third = jax.random.split(key, 3)
    position = jnp.arange(D, dtype=jnp.float32) / D
    column_scale = 0.4 * jnp.exp(position * math.log(3.0)) * jnp.exp(jax.random.uniform(second, (D,), jnp.float32, 0.0, math.log(3.3)))
    row_scale = jnp.exp(jax.random.uniform(third, (L, 1), jnp.float32, math.log(0.3), math.log(3.0)))
    base = jax.random.truncated_normal(first, -4.0, 4.0, (L, D), jnp.float32)
    return base * row_scale * column_scale[None, :]


def level_of(rng, dims, cuts, least, largest):
    gain = 1.0
    for dim, shards_of in cuts:
        steps = jax.random.uniform(jax.random.fold_in(jax.random.fold_in(rng, 6), dim), (shards_of,), jnp.float32, least / len(cuts), largest / len(cuts))
        gain = gain * jnp.repeat(jnp.exp(steps), dims[dim] // shards_of).reshape((-1,) + (1,) * (len(dims) - 1 - dim))
    return gain


def normal_values(stream_key, extent, width, bound, shards=(), held_as=jnp.bfloat16):
    gain = level_of(stream_key, extent, shards, -0.22, 0.18) if shards else 1.0
    entries = jax.random.normal(stream_key, extent, jnp.float32) * width * gain
    return jnp.minimum(jnp.maximum(entries, -bound), bound).astype(held_as)


def setup_inputs(seed: int = 0, part: int = 0) -> dict:
    keys = jax.random.split(jax.random.key(seed), 7)
    part_splits = jax.random.split(jax.random.fold_in(keys[6], part), 7)
    residual_in = draw_residual_in(jax.random.fold_in(jax.random.fold_in(keys[6], part), 71), part)
    norm_gain = jnp.clip(1.0 + 0.18 * jax.random.normal(keys[1], (D,), jnp.float32), 0.1, 1.9)
    in_weight = normal_values(keys[2], (3, D, CH), D ** -0.5, 0.09375, ((1, 4), (2, 4)))
    short_taps = normal_values(keys[3], (3, TAPS, CH), 0.6, 3.0, ((2, 4),), jnp.float32)
    long_filter = normal_values(keys[4], (CH, L), L ** -0.5, 0.25, ((0, 16),), jnp.float32)
    out_weight = normal_values(keys[5], (D, CH), CH ** -0.5, 0.125, ((0, 4), (1, 4)))
    return {"residual_in": residual_in, "norm_gain": norm_gain, "in_weight": in_weight, "short_taps": short_taps, "long_filter": long_filter, "out_weight": out_weight}


def reference(residual_in, norm_gain, in_weight, short_taps, long_filter, out_weight):
    mean_sq = lax.optimization_barrier(jnp.mean(residual_in * residual_in, axis=1, keepdims=True))
    normed = (residual_in * lax.rsqrt(mean_sq + 1e-05) * norm_gain).astype(jnp.bfloat16)
    projected = jnp.einsum('ld,sdc->scl', normed.astype(jnp.float32), in_weight.astype(jnp.float32), precision=lax.Precision.HIGHEST)
    reach = TAPS - 1
    padded = jnp.pad(projected, ((0, 0), (0, 0), (reach, 0)))
    mixed = short_taps[:, 0, :, None] * projected
    for offset in range(1, TAPS):
        mixed = mixed + short_taps[:, offset, :, None] * padded[:, :, reach - offset:reach - offset + L]
    query = mixed[0]
    product_kv = mixed[1] * mixed[2]
    spectrum = jnp.fft.rfft(product_kv, n=2 * L, axis=1) * jnp.fft.rfft(long_filter, n=2 * L, axis=1)
    conv = jnp.fft.irfft(spectrum, n=2 * L, axis=1)[:, :L].astype(jnp.float32)
    gated = (query * conv).astype(jnp.bfloat16)
    block_width = CH // N_TENSOR
    summed = jnp.zeros((L, D), jnp.float32)
    for block in range(N_TENSOR):
        part_gated = gated[block * block_width:(block + 1) * block_width].astype(jnp.float32)
        part_weight = out_weight[:, block * block_width:(block + 1) * block_width].astype(jnp.float32)
        term = jnp.einsum('cl,dc->ld', part_gated, part_weight, precision=lax.Precision.HIGHEST)
        rounded = lax.optimization_barrier(term.astype(jnp.bfloat16))
        summed = summed + rounded.astype(jnp.float32)
    return residual_in + summed
```

```python
import numpy as np

import jax
import jax.numpy as jnp
from jax import lax
from jax.sharding import PartitionSpec as P

EPSILON = 1e-05
BLOCK = 512


def pick(stacked, index):
    return lax.dynamic_index_in_dim(stacked, index, 0, keepdims=False)


def hop(value, axis, mask):
    count = lax.axis_size(axis)
    return lax.ppermute(value, axis, [(a, a ^ mask) for a in range(count)])


def exchange(blocks, axis):
    me = lax.axis_index(axis)
    count = lax.axis_size(axis)
    got = [pick(blocks, me)]
    got += [hop(pick(blocks, me ^ mask), axis, mask) for mask in range(1, count)]
    got = jnp.stack(got)
    return jnp.stack([pick(got, me ^ source) for source in range(count)])


def gather(value, axis):
    me = lax.axis_index(axis)
    count = lax.axis_size(axis)
    held = value[None]
    mask = count // 2
    while mask:
        held = jnp.concatenate([held, hop(held, axis, mask)])
        mask //= 2
    codes = [0]
    mask = count // 2
    while mask:
        codes += [code ^ mask for code in codes]
        mask //= 2
    slot_of = {code: slot for slot, code in enumerate(codes)}
    slots = jnp.array([slot_of[code] for code in range(count)], jnp.int32)
    return jnp.stack([pick(held, slots[me ^ source]) for source in range(count)])


def sum_over_seq(partial_for, axis="seq"):
    count = lax.axis_size(axis)
    parts = {mask: partial_for(mask) for mask in range(count)}
    total = parts[0]
    low = {mask: parts[mask].astype(jnp.bfloat16) for mask in range(1, count)}
    if count != 4:
        for mask in range(1, count):
            total = total + hop(low[mask], axis, mask).astype(jnp.float32)
        return total
    relayed = lax.ppermute(low[3], axis, [(0, 1), (3, 2)])
    far = lax.ppermute(low[2], axis, [(0, 2), (3, 1)])
    near = hop(low[1], axis, 1)
    middle = lax.ppermute(low[3], axis, [(1, 2), (2, 1)])
    merged = (parts[2] + relayed.astype(jnp.float32)).astype(jnp.bfloat16)
    merged = lax.ppermute(merged, axis, [(1, 3), (2, 0)])
    for term in (near, middle, far, merged):
        total = total + term.astype(jnp.float32)
    return total


def tables(block):
    odd = 2 * np.arange(block)[:, None] + 1
    theta = (odd * np.arange(2 * block)[None, :] % (4 * block)) * (np.pi / (2 * block))
    return np.concatenate([np.cos(theta), np.sin(theta)]).astype(np.float32)


def causal_convolution(signal, taps):
    channels, length = signal.shape
    block = min(length, BLOCK)
    count = length // block
    table = jnp.asarray(tables(block))
    forward = table[:, :block]

    def spectrum(rows):
        cut = rows.reshape(channels * count, block)
        both = jnp.einsum("ct,ft->cf", cut, forward, precision=lax.Precision.HIGH)
        both = both.reshape(channels, count, 2 * block)
        return both[:, :, :block], both[:, :, block:]

    taps_cos, taps_sin = spectrum(taps)
    cos, sin = spectrum(signal)
    outputs = []
    spill = None
    for last in range(count):
        real = imag = 0.0
        for one in range(last + 1):
            other = last - one
            real = real + cos[:, one] * taps_cos[:, other] - sin[:, one] * taps_sin[:, other]
            imag = imag + cos[:, one] * taps_sin[:, other] + sin[:, one] * taps_cos[:, other]
        both = jnp.concatenate([real, imag], axis=1)
        reach = block if last == count - 1 else 2 * block
        back = jnp.einsum("cf,ft->ct", both, table[:, :reach], precision=lax.Precision.HIGH) / block
        here = back[:, :block]
        outputs.append(here if spill is None else here + spill)
        spill = back[:, block:]
    return outputs[0] if count == 1 else jnp.concatenate(outputs, axis=1)


def shards(residual_in, norm_gain, in_weight, short_taps, long_filter, out_weight):
    seq, tensor = lax.axis_size("seq"), lax.axis_size("tensor")
    z = lax.axis_index("seq")
    rows, width = residual_in.shape
    streams, depth, channels = in_weight.shape
    model = width * tensor
    sub = rows // tensor
    own = channels // seq
    length = rows * seq

    whole = exchange(residual_in.astype(jnp.bfloat16).reshape(tensor, sub, width), "tensor")
    whole = whole.transpose(1, 0, 2).reshape(sub, model).astype(jnp.float32)
    mean_sq = jnp.mean(whole * whole, axis=1, keepdims=True)
    normed = (whole * lax.rsqrt(mean_sq + EPSILON) * norm_gain).astype(jnp.bfloat16)
    normed = exchange(normed.reshape(sub, seq, depth).transpose(1, 0, 2), "seq")
    normed = gather(normed, "tensor")
    normed = normed.transpose(1, 0, 2, 3).reshape(length, depth)

    def projected_for(mask):
        weight = lax.dynamic_slice_in_dim(in_weight, (z ^ mask) * own, own, 2)
        return jnp.einsum("rd,sdc->scr", normed, weight, preferred_element_type=jnp.float32)

    projected = sum_over_seq(projected_for)
    taps = lax.dynamic_slice_in_dim(short_taps, z * own, own, 2)
    reach = taps.shape[1] - 1
    padded = jnp.pad(projected, ((0, 0), (0, 0), (reach, 0)))
    mixed = taps[:, 0, :, None] * projected
    for offset in range(1, reach + 1):
        mixed = mixed + taps[:, offset, :, None] * padded[:, :, reach - offset : reach - offset + length]
    conv = causal_convolution(mixed[1] * mixed[2], long_filter)
    gated = (mixed[0] * conv).astype(jnp.bfloat16)

    got = [gated] + [hop(gated, "seq", mask) for mask in range(1, seq)]
    turned = [lax.dynamic_slice_in_dim(out_weight, (z ^ mask) * own, own, 1) for mask in range(seq)]
    terms = jnp.einsum(
        "cr,nc->rn",
        jnp.concatenate(got, axis=0),
        jnp.concatenate(turned, axis=1),
        preferred_element_type=jnp.float32,
    ).astype(jnp.bfloat16)

    held = terms.reshape(seq, tensor, sub, depth)
    t = lax.axis_index("tensor")
    mask = 1
    lead = tensor
    while mask < tensor:
        held = held.reshape(seq, lead // 2, 2, sub, depth)
        bit = (t // mask) % 2
        give = lax.dynamic_index_in_dim(held, 1 - bit, 2, keepdims=False)
        keep = lax.dynamic_index_in_dim(held, bit, 2, keepdims=False)
        came = hop(give, "tensor", mask)
        held = (keep.astype(jnp.float32) + came.astype(jnp.float32)).astype(jnp.bfloat16)
        lead //= 2
        mask *= 2
    back = exchange(held.reshape(seq, sub, depth), "seq")
    back = back.transpose(1, 0, 2).reshape(sub, tensor, width).transpose(1, 0, 2)
    summed = exchange(back, "tensor").reshape(rows, width)
    return residual_in + summed.astype(jnp.float32)


def solution(mesh):
    return jax.shard_map(
        shards,
        mesh=mesh,
        in_specs=(
            P(("groups", "seq"), "tensor"),
            P(),
            P(None, "seq", "tensor"),
            P(None, None, "tensor"),
            P(("tensor", "seq"), None),
            P("seq", "tensor"),
        ),
        out_specs=P(("groups", "seq"), "tensor"),
        check_vma=False,
    )
```

```python
import numpy as np

import jax
import jax.numpy as jnp
from jax import lax
from jax.sharding import PartitionSpec as P

EPSILON = 1e-05
BLOCK = 512


def pick(stacked, index):
    return lax.dynamic_index_in_dim(stacked, index, 0, keepdims=False)


def hop(value, axis, mask):
    count = lax.axis_size(axis)
    return lax.ppermute(value, axis, [(a, a ^ mask) for a in range(count)])


def exchange(blocks, axis):
    me = lax.axis_index(axis)
    count = lax.axis_size(axis)
    got = [pick(blocks, me)]
    got += [hop(pick(blocks, me ^ mask), axis, mask) for mask in range(1, count)]
    got = jnp.stack(got)
    return jnp.stack([pick(got, me ^ source) for source in range(count)])


def spread(value, axis):
    parts = {0: value}
    mask = lax.axis_size(axis) // 2
    while mask:
        parts.update({slot ^ mask: hop(part, axis, mask) for slot, part in parts.items()})
        mask //= 2
    return parts


def collect(parts, axis):
    parts = dict(parts)
    mask = 1
    while mask < lax.axis_size(axis):
        for slot in sorted(parts, reverse=True):
            if slot & mask:
                came = hop(parts.pop(slot).astype(jnp.bfloat16), axis, mask)
                parts[slot ^ mask] = parts[slot ^ mask] + came.astype(jnp.float32)
        mask *= 2
    return parts[0]


def sum_over_seq(rows, weights):
    narrow = weights[0].shape[1] % 128 != 0

    def product(mask):
        form = "rd,dn->nr" if narrow else "rd,dn->rn"
        return jnp.einsum(form, rows, weights[mask], preferred_element_type=jnp.float32)

    sent = {mask: product(mask).astype(jnp.bfloat16) for mask in range(1, len(weights))}
    came = [hop(sent[mask], "seq", mask) for mask in sent]
    total = product(0)
    for term in came:
        total = total + term.astype(jnp.float32)
    return total.T if narrow else total


def tables(block):
    odd = 2 * np.arange(block)[:, None] + 1
    theta = (odd * np.arange(2 * block)[None, :] % (4 * block)) * (np.pi / (2 * block))
    return np.concatenate([np.cos(theta), np.sin(theta)]).astype(np.float32)


def causal_convolution(signal, taps):
    length, channels = signal.shape
    block = min(length, BLOCK)
    count = length // block
    table = jnp.asarray(tables(block))
    forward = table[:, :block]
    taps_all = jnp.einsum("ft,ckt->kfc", forward, taps.reshape(channels, count, block), precision=lax.Precision.HIGH)
    taps_cos, taps_sin = taps_all[:, :block], taps_all[:, block:]
    both = jnp.stack(
        [
            jnp.einsum("ft,tc->fc", forward, signal[one * block : (one + 1) * block], precision=lax.Precision.HIGH)
            for one in range(count)
        ]
    )
    cos, sin = both[:, :block], both[:, block:]
    outputs = []
    spill = None
    for last in range(count):
        real = imag = 0.0
        for one in range(last + 1):
            other = last - one
            real = real + cos[one] * taps_cos[other] - sin[one] * taps_sin[other]
            imag = imag + cos[one] * taps_sin[other] + sin[one] * taps_cos[other]
        both = jnp.concatenate([real, imag])
        reach = block if last == count - 1 else 2 * block
        back = jnp.einsum("ft,fc->tc", table[:, :reach], both, precision=lax.Precision.HIGH) / block
        here = back[:block]
        outputs.append(here if spill is None else here + spill)
        spill = back[block:]
    return outputs[0] if count == 1 else jnp.concatenate(outputs)


def shards(residual_in, norm_gain, in_weight, short_taps, long_filter, out_weight):
    seq, tensor = lax.axis_size("seq"), lax.axis_size("tensor")
    z, t = lax.axis_index("seq"), lax.axis_index("tensor")
    rows, width = residual_in.shape
    streams, depth, channels = in_weight.shape
    model = width * tensor
    sub = rows // tensor
    own = channels // seq
    length = rows * seq
    slots = range(tensor)

    whole = exchange(residual_in.astype(jnp.bfloat16).reshape(tensor, sub, width), "tensor")
    in_parts, out_parts = [], []
    for mask in range(seq):
        part = lax.dynamic_slice_in_dim(in_weight, (z ^ mask) * own, own, 2)
        in_parts.append(part.transpose(1, 0, 2).reshape(depth, streams * own))
        out_parts.append(lax.dynamic_slice_in_dim(out_weight, (z ^ mask) * own, own, 1))
    out_turned = jnp.concatenate(out_parts, axis=1)
    taps = lax.dynamic_slice_in_dim(short_taps, z * own, own, 2)
    whole = whole.transpose(1, 0, 2).reshape(sub, model).astype(jnp.float32)
    mean_sq = jnp.mean(whole * whole, axis=1, keepdims=True)
    normed = (whole * lax.rsqrt(mean_sq + EPSILON) * norm_gain).astype(jnp.bfloat16)
    normed = exchange(normed.reshape(sub, seq, depth).transpose(1, 0, 2), "seq")
    parts = spread(normed.reshape(seq * sub, depth), "tensor")
    early = jnp.concatenate([parts[slot] for slot in slots[:2]])
    late = jnp.concatenate([parts[slot] for slot in slots[2:]])
    sums = [sum_over_seq(early, in_parts), sum_over_seq(late, in_parts)]
    projected = jnp.concatenate(sums).reshape(tensor, seq, sub, streams * own)
    projected = jnp.stack([pick(projected, t ^ slot) for slot in slots], axis=1)
    projected = projected.reshape(length, streams * own)

    reach = taps.shape[1] - 1
    padded = jnp.pad(projected, ((reach, 0), (0, 0)))
    mixed = 0.0
    for offset in range(reach + 1):
        row = taps[:, offset].reshape(1, streams * own)
        mixed = mixed + row * padded[reach - offset : reach - offset + length]
    query, key, value = (mixed[:, s * own : (s + 1) * own] for s in range(streams))
    conv = causal_convolution(key * value, long_filter)
    gated = (query * conv).astype(jnp.bfloat16).reshape(seq, tensor, sub, own)
    gated = jnp.stack([lax.dynamic_index_in_dim(gated, t ^ slot, 1, keepdims=False) for slot in slots])
    gated = gated.reshape(length, own)

    got = [gated] + [hop(gated, "seq", mask) for mask in range(1, seq)]
    got = jnp.concatenate(got, axis=1)
    terms = {}
    for slot in slots:
        chosen = got[slot * seq * sub : (slot + 1) * seq * sub]
        terms[slot] = jnp.einsum("rc,nc->rn", chosen, out_turned, preferred_element_type=jnp.float32)
    held = collect(terms, "tensor").astype(jnp.bfloat16)
    back = exchange(held.reshape(seq, sub, depth), "seq")
    back = back.transpose(1, 0, 2).reshape(sub, tensor, width).transpose(1, 0, 2)
    summed = exchange(back, "tensor").reshape(rows, width)
    return residual_in + summed.astype(jnp.float32)


def solution(mesh):
    return jax.shard_map(
        shards,
        mesh=mesh,
        in_specs=(
            P(("groups", "seq"), "tensor"),
            P(),
            P(None, "seq", "tensor"),
            P(None, None, "tensor"),
            P(("tensor", "seq"), None),
            P("seq", "tensor"),
        ),
        out_specs=P(("groups", "seq"), "tensor"),
        check_vma=False,
    )
```

```python
import numpy as np

import jax
import jax.numpy as jnp
from jax import lax
from jax.sharding import PartitionSpec as P

EPSILON = 1e-05
BLOCK = 512


def pick(stacked, index):
    return lax.dynamic_index_in_dim(stacked, index, 0, keepdims=False)


def hop(value, axis, mask):
    count = lax.axis_size(axis)
    return lax.ppermute(value, axis, [(a, a ^ mask) for a in range(count)])


def exchange(blocks, axis):
    me = lax.axis_index(axis)
    count = lax.axis_size(axis)
    got = [pick(blocks, me)]
    got += [hop(pick(blocks, me ^ mask), axis, mask) for mask in range(1, count)]
    got = jnp.stack(got)
    return jnp.stack([pick(got, me ^ source) for source in range(count)])


def spread(value, axis):
    parts = {0: value}
    mask = lax.axis_size(axis) // 2
    while mask:
        parts.update({slot ^ mask: hop(part, axis, mask) for slot, part in parts.items()})
        mask //= 2
    return parts


def fold(parts, axis, masks):
    parts = dict(parts)
    for mask in masks:
        for slot in sorted(parts, reverse=True):
            if slot & mask:
                came = hop(parts.pop(slot).astype(jnp.bfloat16), axis, mask)
                parts[slot ^ mask] = parts[slot ^ mask] + came.astype(jnp.float32)
    return parts


def sum_over_seq(rows, weight_of):
    count = lax.axis_size("seq")
    narrow = weight_of(0).shape[2] % 128 != 0

    def product(mask):
        form = "rd,sdc->scr" if narrow else "rd,sdc->src"
        return jnp.einsum(form, rows, weight_of(mask), preferred_element_type=jnp.float32)

    sent = {mask: product(mask).astype(jnp.bfloat16) for mask in range(1, count)}
    came = [hop(sent[mask], "seq", mask) for mask in sent]
    total = product(0)
    for term in came:
        total = total + term.astype(jnp.float32)
    return total.transpose(0, 2, 1) if narrow else total


def tables(block):
    odd = 2 * np.arange(block)[:, None] + 1
    theta = (odd * np.arange(2 * block)[None, :] % (4 * block)) * (np.pi / (2 * block))
    return np.concatenate([np.cos(theta), np.sin(theta)]).astype(np.float32)


def causal_convolution(signal, taps):
    length, channels = signal.shape
    block = min(length, BLOCK)
    count = length // block
    table = jnp.asarray(tables(block))
    forward = table[:, :block]
    taps_all = jnp.einsum("ft,ckt->kfc", forward, taps.reshape(channels, count, block), precision=lax.Precision.HIGH)
    taps_cos, taps_sin = taps_all[:, :block], taps_all[:, block:]
    both = jnp.stack(
        [
            jnp.einsum("ft,tc->fc", forward, signal[one * block : (one + 1) * block], precision=lax.Precision.HIGH)
            for one in range(count)
        ]
    )
    cos, sin = both[:, :block], both[:, block:]
    outputs = []
    spill = None
    for last in range(count):
        real = imag = 0.0
        for one in range(last + 1):
            other = last - one
            real = real + cos[one] * taps_cos[other] - sin[one] * taps_sin[other]
            imag = imag + cos[one] * taps_sin[other] + sin[one] * taps_cos[other]
        both = jnp.concatenate([real, imag])
        reach = block if last == count - 1 else 2 * block
        back = jnp.einsum("ft,fc->tc", table[:, :reach], both, precision=lax.Precision.HIGH) / block
        here = back[:block]
        outputs.append(here if spill is None else here + spill)
        spill = back[block:]
    return outputs[0] if count == 1 else jnp.concatenate(outputs)


def shards(residual_in, norm_gain, in_weight, short_taps, long_filter, out_weight):
    seq, tensor = lax.axis_size("seq"), lax.axis_size("tensor")
    z, t = lax.axis_index("seq"), lax.axis_index("tensor")
    rows, width = residual_in.shape
    streams, depth, channels = in_weight.shape
    model = width * tensor
    sub = rows // tensor
    own = channels // seq
    length = rows * seq
    slots = range(tensor)

    whole = exchange(residual_in.astype(jnp.bfloat16).reshape(tensor, sub, width), "tensor")
    def in_part(mask):
        return lax.dynamic_slice_in_dim(in_weight, (z ^ mask) * own, own, 2)

    out_parts = [lax.dynamic_slice_in_dim(out_weight, (z ^ mask) * own, own, 1) for mask in range(seq)]
    out_turned = jnp.concatenate(out_parts, axis=1)
    taps = lax.dynamic_slice_in_dim(short_taps, z * own, own, 2)
    whole = whole.transpose(1, 0, 2).reshape(sub, model).astype(jnp.float32)
    mean_sq = jnp.mean(whole * whole, axis=1, keepdims=True)
    normed = (whole * lax.rsqrt(mean_sq + EPSILON) * norm_gain).astype(jnp.bfloat16)
    normed = exchange(normed.reshape(sub, seq, depth).transpose(1, 0, 2), "seq")
    parts = spread(normed.reshape(seq * sub, depth), "tensor")
    early = jnp.concatenate([parts[slot] for slot in slots[:2]])
    late = jnp.concatenate([parts[slot] for slot in slots[2:]])
    sums = [sum_over_seq(early, in_part), sum_over_seq(late, in_part)]
    projected = jnp.concatenate(sums, axis=1).reshape(streams, tensor, seq, sub, own)
    projected = jnp.stack([lax.dynamic_index_in_dim(projected, t ^ slot, 1, keepdims=False) for slot in slots], axis=2)
    projected = projected.reshape(streams, length, own)

    reach = taps.shape[1] - 1
    padded = jnp.pad(projected, ((0, 0), (reach, 0), (0, 0)))
    mixed = 0.0
    for offset in range(reach + 1):
        mixed = mixed + taps[:, offset, None] * padded[:, reach - offset : reach - offset + length]
    query, key, value = mixed
    conv = causal_convolution(key * value, long_filter)
    gated = (query * conv).astype(jnp.bfloat16).reshape(seq, tensor, sub, own)
    gated = jnp.stack([lax.dynamic_index_in_dim(gated, t ^ slot, 1, keepdims=False) for slot in slots])

    half = tensor // 2
    lower = [1 << bit for bit in range(half.bit_length() - 1)]
    held = None
    for chosen in (slots[half:], slots[:half]):
        piece = jnp.concatenate([gated[slot].reshape(seq * sub, own) for slot in chosen])
        got = [piece] + [hop(piece, "seq", mask) for mask in range(1, seq)]
        got = jnp.concatenate(got, axis=1)
        terms = {}
        for place, slot in enumerate(chosen):
            terms[slot] = jnp.einsum(
                "rc,nc->rn",
                got[place * seq * sub : (place + 1) * seq * sub],
                out_turned,
                preferred_element_type=jnp.float32,
            )
        terms = fold(terms, "tensor", lower)
        if held is None:
            held = hop(terms[half].astype(jnp.bfloat16), "tensor", half)
        else:
            held = (terms[0] + held.astype(jnp.float32)).astype(jnp.bfloat16)
    back = exchange(held.reshape(seq, sub, depth), "seq")
    back = back.transpose(1, 0, 2).reshape(sub, tensor, width).transpose(1, 0, 2)
    summed = exchange(back, "tensor").reshape(rows, width)
    return residual_in + summed.astype(jnp.float32)


def solution(mesh):
    return jax.shard_map(
        shards,
        mesh=mesh,
        in_specs=(
            P(("groups", "seq"), "tensor"),
            P(),
            P(None, "seq", "tensor"),
            P(None, None, "tensor"),
            P(("tensor", "seq"), None),
            P("seq", "tensor"),
        ),
        out_specs=P(("groups", "seq"), "tensor"),
        check_vma=False,
    )
```

```python
import functools

import jax
import jax.numpy as jnp
import numpy as np
from jax import lax
from jax.experimental import pallas as pl
from jax.experimental.pallas import tpu as pltpu
from jax.sharding import PartitionSpec as P

EPSILON = 1e-05
BLOCK = 512


def pick(stacked, index):
    return lax.dynamic_index_in_dim(stacked, index, 0, keepdims=False)


def hop(value, axis, mask):
    count = lax.axis_size(axis)
    return lax.ppermute(value, axis, [(a, a ^ mask) for a in range(count)])


def exchange(blocks, axis):
    me = lax.axis_index(axis)
    count = lax.axis_size(axis)
    got = [pick(blocks, me)]
    got += [hop(pick(blocks, me ^ mask), axis, mask) for mask in range(1, count)]
    got = jnp.stack(got)
    return jnp.stack([pick(got, me ^ source) for source in range(count)])


def spread(value, axis):
    parts = {0: value}
    mask = lax.axis_size(axis) // 2
    while mask:
        parts.update({slot ^ mask: hop(part, axis, mask) for slot, part in parts.items()})
        mask //= 2
    return parts


def fold(parts, axis, masks):
    parts = dict(parts)
    for mask in masks:
        for slot in sorted(parts, reverse=True):
            if slot & mask:
                came = hop(parts.pop(slot).astype(jnp.bfloat16), axis, mask)
                parts[slot ^ mask] = parts[slot ^ mask] + came.astype(jnp.float32)
    return parts


def sum_over_seq(rows, weight_of):
    count = lax.axis_size("seq")
    narrow = weight_of(0).shape[2] % 128 != 0

    def product(mask):
        form = "rd,sdc->scr" if narrow else "rd,sdc->src"
        return jnp.einsum(form, rows, weight_of(mask), preferred_element_type=jnp.float32)

    sent = {mask: product(mask).astype(jnp.bfloat16) for mask in range(1, count)}
    came = [hop(sent[mask], "seq", mask) for mask in sent]
    if narrow:
        return [term.transpose(0, 2, 1) for term in [product(0)] + came]
    return [product(0)] + came


def tables(block):
    odd = 2 * np.arange(block)[:, None] + 1
    theta = (odd * np.arange(2 * block)[None, :] % (4 * block)) * (np.pi / (2 * block))
    return np.concatenate([np.cos(theta), np.sin(theta)]).astype(np.float32)


def causal_convolution(signal, taps):
    length, channels = signal.shape
    block = min(length, BLOCK)
    count = length // block
    table = jnp.asarray(tables(block))
    forward = table[:, :block]
    taps_all = jnp.einsum("ft,ckt->kfc", forward, taps.reshape(channels, count, block), precision=lax.Precision.HIGH)
    taps_cos, taps_sin = taps_all[:, :block], taps_all[:, block:]
    both = jnp.stack(
        [
            jnp.einsum("ft,tc->fc", forward, signal[one * block : (one + 1) * block], precision=lax.Precision.HIGH)
            for one in range(count)
        ]
    )
    cos, sin = both[:, :block], both[:, block:]
    outputs = []
    spill = None
    for last in range(count):
        real = imag = 0.0
        for one in range(last + 1):
            other = last - one
            real = real + cos[one] * taps_cos[other] - sin[one] * taps_sin[other]
            imag = imag + cos[one] * taps_sin[other] + sin[one] * taps_cos[other]
        both = jnp.concatenate([real, imag])
        reach = block if last == count - 1 else 2 * block
        back = jnp.einsum("ft,fc->tc", table[:, :reach], both, precision=lax.Precision.HIGH) / block
        here = back[:block]
        outputs.append(here if spill is None else here + spill)
        spill = back[block:]
    return outputs[0] if count == 1 else jnp.concatenate(outputs)


def halves(value):
    high = value.astype(jnp.bfloat16)
    return high, (value - high.astype(jnp.float32)).astype(jnp.bfloat16)


def split_tables(block):
    table = tables(block)[:, :block]
    out = []
    for part in (table, table.T / np.float32(block)):
        high = part.astype(jnp.bfloat16)
        out += [high, (part - high.astype(np.float32)).astype(jnp.bfloat16)]
    return out


def wide_dot(high, low, value, dims):
    dot = functools.partial(lax.dot_general, dimension_numbers=(dims, ((), ())), preferred_element_type=jnp.float32)
    upper, lower = halves(value)
    return dot(high, upper) + dot(high, lower) + dot(low, upper)


def filter_kernel(high_ref, low_ref, taps_ref, out_ref):
    out_ref[...] = wide_dot(high_ref[...], low_ref[...], taps_ref[...], ((1,), (1,)))


def local_kernel(groups, seq, sub, t_ref, taps_ref, spectrum_ref, *refs):
    count = seq * len(groups)
    terms, refs = refs[:count], refs[count:]
    table_refs, outs, (proj, gated, fore_high, fore_low, back_high, back_low, sems) = refs[:4], refs[4:6], refs[6:]
    held = (fore_high, fore_low, back_high, back_low)
    copies = [pltpu.make_async_copy(table_refs[i], held[i], sems.at[i]) for i in range(4)]
    for copy in copies:
        copy.start()
    t = t_ref[0]
    length = gated.shape[0]
    shard = length // seq
    tensor = shard // sub

    def place(slot, source, lead):
        return pl.ds(pl.multiple_of(lead + source * shard + (t ^ slot) * sub, 8), sub)

    proj[:, :8] = jnp.zeros((proj.shape[0], 8, proj.shape[2]), jnp.float32)
    for group, slots in enumerate(groups):
        mine = terms[group * seq : (group + 1) * seq]
        for position, slot in enumerate(slots):
            for source in range(seq):
                rows = pl.ds((position * seq + source) * sub, sub)
                total = mine[0][:, rows]
                for term in mine[1:]:
                    total = total + term[:, rows].astype(jnp.float32)
                proj[:, place(slot, source, 8)] = total

    def mixed(stream):
        total = taps_ref[stream, 0:1] * proj[stream, pl.ds(8, length)]
        for offset in range(1, taps_ref.shape[1]):
            total = total + taps_ref[stream, offset : offset + 1] * proj[stream, pl.ds(8 - offset, length)]
        return total

    signal = mixed(1) * mixed(2)
    copies[0].wait()
    copies[1].wait()
    both = wide_dot(fore_high[...], fore_low[...], signal, ((1,), (0,)))
    cos, sin = both[:length], both[length:]
    taps_cos, taps_sin = spectrum_ref[:length], spectrum_ref[length:]
    both = jnp.concatenate([cos * taps_cos - sin * taps_sin, cos * taps_sin + sin * taps_cos])
    copies[2].wait()
    copies[3].wait()
    gated[...] = mixed(0) * wide_dot(back_high[...], back_low[...], both, ((1,), (0,)))
    for slot in range(tensor):
        out = outs[slot // (tensor // 2)]
        for source in range(seq):
            row = ((slot % (tensor // 2)) * seq + source) * sub
            out[row : row + sub] = gated[place(slot, source, 0)].astype(jnp.bfloat16)


def local_stage(groups, terms, taps, long_filter, t, seq, sub):
    own, length = long_filter.shape
    wide = split_tables(length)
    vmem = pl.BlockSpec(memory_space=pltpu.VMEM)
    spectrum = pl.pallas_call(
        filter_kernel,
        out_shape=jax.ShapeDtypeStruct((2 * length, own), jnp.float32),
        in_specs=[vmem] * 3,
        out_specs=vmem,
        name="filter_spectrum",
        cost_estimate=pl.CostEstimate(flops=12 * length * length * own, bytes_accessed=4 * length * length, transcendentals=0),
    )(*wide[:2], long_filter)
    flat = [term for group in terms for term in group]
    lines = length // 2
    table_shape = (2 * length, length)
    return pl.pallas_call(
        functools.partial(local_kernel, groups, seq, sub),
        out_shape=[jax.ShapeDtypeStruct((lines, own), jnp.bfloat16)] * 2,
        in_specs=[pl.BlockSpec(memory_space=pltpu.SMEM)]
        + [vmem] * (2 + len(flat))
        + [pl.BlockSpec(memory_space=pl.ANY)] * 4,
        out_specs=[vmem] * 2,
        scratch_shapes=[
            pltpu.VMEM((3, length + 8, own), jnp.float32),
            pltpu.VMEM((length, own), jnp.float32),
            pltpu.VMEM(table_shape, jnp.bfloat16),
            pltpu.VMEM(table_shape, jnp.bfloat16),
            pltpu.VMEM(table_shape[::-1], jnp.bfloat16),
            pltpu.VMEM(table_shape[::-1], jnp.bfloat16),
            pltpu.SemaphoreType.DMA((4,)),
        ],
        name="filters",
        cost_estimate=pl.CostEstimate(flops=24 * length * length * own, bytes_accessed=8 * length * length, transcendentals=0),
    )(t.reshape(1).astype(jnp.int32), taps, spectrum, *flat, *wide)


def plain_stage(terms, taps, long_filter, t, seq, sub):
    streams, _, own = terms[0][0].shape
    length = long_filter.shape[1]
    tensor = length // (seq * sub)
    sums = []
    for group in terms:
        total = group[0]
        for term in group[1:]:
            total = total + term.astype(jnp.float32)
        sums.append(total)
    slots = range(tensor)
    projected = jnp.concatenate(sums, axis=1).reshape(streams, tensor, seq, sub, own)
    projected = jnp.stack([lax.dynamic_index_in_dim(projected, t ^ slot, 1, keepdims=False) for slot in slots], axis=2)
    projected = projected.reshape(streams, length, own)
    reach = taps.shape[1] - 1
    padded = jnp.pad(projected, ((0, 0), (reach, 0), (0, 0)))
    mixed = 0.0
    for offset in range(reach + 1):
        mixed = mixed + taps[:, offset, None] * padded[:, reach - offset : reach - offset + length]
    query, key, value = mixed
    conv = causal_convolution(key * value, long_filter)
    gated = (query * conv).astype(jnp.bfloat16).reshape(seq, tensor, sub, own)
    gated = [lax.dynamic_index_in_dim(gated, t ^ slot, 1, keepdims=False) for slot in slots]
    return [rows.reshape(seq * sub, own) for rows in gated]


def shards(residual_in, norm_gain, in_weight, short_taps, long_filter, out_weight):
    seq, tensor = lax.axis_size("seq"), lax.axis_size("tensor")
    z, t = lax.axis_index("seq"), lax.axis_index("tensor")
    rows, width = residual_in.shape
    streams, depth, channels = in_weight.shape
    model = width * tensor
    sub = rows // tensor
    own = channels // seq
    length = rows * seq
    slots = range(tensor)

    whole = exchange(residual_in.astype(jnp.bfloat16).reshape(tensor, sub, width), "tensor")
    def in_part(mask):
        return lax.dynamic_slice_in_dim(in_weight, (z ^ mask) * own, own, 2)

    out_parts = [lax.dynamic_slice_in_dim(out_weight, (z ^ mask) * own, own, 1) for mask in range(seq)]
    out_turned = jnp.concatenate(out_parts, axis=1)
    taps = lax.dynamic_slice_in_dim(short_taps, z * own, own, 2)
    whole = whole.transpose(1, 0, 2).reshape(sub, model).astype(jnp.float32)
    mean_sq = jnp.mean(whole * whole, axis=1, keepdims=True)
    normed = (whole * lax.rsqrt(mean_sq + EPSILON) * norm_gain).astype(jnp.bfloat16)
    normed = exchange(normed.reshape(sub, seq, depth).transpose(1, 0, 2), "seq")
    parts = spread(normed.reshape(seq * sub, depth), "tensor")
    groups = (tuple(slots[:1]), tuple(slots[1:]))
    terms = []
    for group in groups:
        terms.append(sum_over_seq(jnp.concatenate([parts[slot] for slot in group]), in_part))
    half = tensor // 2
    if own % 128 == 0 and length <= BLOCK and sub % 16 == 0:
        lower_gated, upper_gated = local_stage(groups, terms, taps, long_filter, t, seq, sub)
    else:
        gated = plain_stage(terms, taps, long_filter, t, seq, sub)
        lower_gated = jnp.concatenate(gated[:half])
        upper_gated = jnp.concatenate(gated[half:])

    lower = [1 << bit for bit in range(half.bit_length() - 1)]
    held = None
    for chosen, piece in ((slots[half:], upper_gated), (slots[:half], lower_gated)):
        got = [piece] + [hop(piece, "seq", mask) for mask in range(1, seq)]
        got = jnp.concatenate(got, axis=1)
        terms = {}
        for place, slot in enumerate(chosen):
            terms[slot] = jnp.einsum(
                "rc,nc->rn",
                got[place * seq * sub : (place + 1) * seq * sub],
                out_turned,
                preferred_element_type=jnp.float32,
            )
        terms = fold(terms, "tensor", lower)
        if held is None:
            held = hop(terms[half].astype(jnp.bfloat16), "tensor", half)
        else:
            held = (terms[0] + held.astype(jnp.float32)).astype(jnp.bfloat16)
    back = exchange(held.reshape(seq, sub, depth), "seq")
    back = back.transpose(1, 0, 2).reshape(sub, tensor, width).transpose(1, 0, 2)
    summed = exchange(back, "tensor").reshape(rows, width)
    return residual_in + summed.astype(jnp.float32)


def solution(mesh):
    return jax.shard_map(
        shards,
        mesh=mesh,
        in_specs=(
            P(("groups", "seq"), "tensor"),
            P(),
            P(None, "seq", "tensor"),
            P(None, None, "tensor"),
            P(("tensor", "seq"), None),
            P("seq", "tensor"),
        ),
        out_specs=P(("groups", "seq"), "tensor"),
        check_vma=False,
    )
```

```python
import functools

import jax
import jax.numpy as jnp
import numpy as np
from jax import lax
from jax.experimental import pallas as pl
from jax.experimental.pallas import tpu as pltpu
from jax.sharding import PartitionSpec as P


EPSILON = 1e-05
BLOCK = 512


def pick(stacked, index):
    return lax.dynamic_index_in_dim(stacked, index, 0, keepdims=False)


def hop(value, axis, mask):
    count = lax.axis_size(axis)
    return lax.ppermute(value, axis, [(a, a ^ mask) for a in range(count)])


def exchange(blocks, axis):
    me = lax.axis_index(axis)
    count = lax.axis_size(axis)
    got = [pick(blocks, me)]
    got += [hop(pick(blocks, me ^ mask), axis, mask) for mask in range(1, count)]
    got = jnp.stack(got)
    return jnp.stack([pick(got, me ^ source) for source in range(count)])


def spread(value, axis):
    parts = {0: value}
    mask = lax.axis_size(axis) // 2
    while mask:
        parts.update({slot ^ mask: hop(part, axis, mask) for slot, part in parts.items()})
        mask //= 2
    return parts


def fold(parts, axis, masks):
    parts = dict(parts)
    for mask in masks:
        for slot in sorted(parts, reverse=True):
            if slot & mask:
                came = hop(parts.pop(slot).astype(jnp.bfloat16), axis, mask)
                parts[slot ^ mask] = parts[slot ^ mask] + came.astype(jnp.float32)
    return parts


def sum_over_seq(rows, weight_of):
    count = lax.axis_size("seq")
    narrow = weight_of(0).shape[2] % 128 != 0

    def product(mask):
        form = "rd,sdc->scr" if narrow else "rd,sdc->src"
        return jnp.einsum(form, rows, weight_of(mask), preferred_element_type=jnp.float32)

    sent = {mask: product(mask).astype(jnp.bfloat16) for mask in range(1, count)}
    came = [hop(sent[mask], "seq", mask) for mask in sent]
    if narrow:
        return [term.transpose(0, 2, 1) for term in [product(0)] + came]
    return [product(0)] + came


def tables(block):
    odd = 2 * np.arange(block)[:, None] + 1
    theta = (odd * np.arange(2 * block)[None, :] % (4 * block)) * (np.pi / (2 * block))
    return np.concatenate([np.cos(theta), np.sin(theta)]).astype(np.float32)


def causal_convolution(signal, taps):
    length, channels = signal.shape
    block = min(length, BLOCK)
    count = length // block
    table = jnp.asarray(tables(block))
    forward = table[:, :block]
    taps_all = jnp.einsum("ft,ckt->kfc", forward, taps.reshape(channels, count, block), precision=lax.Precision.HIGH)
    taps_cos, taps_sin = taps_all[:, :block], taps_all[:, block:]
    both = jnp.stack(
        [
            jnp.einsum("ft,tc->fc", forward, signal[one * block : (one + 1) * block], precision=lax.Precision.HIGH)
            for one in range(count)
        ]
    )
    cos, sin = both[:, :block], both[:, block:]
    outputs = []
    spill = None
    for last in range(count):
        real = imag = 0.0
        for one in range(last + 1):
            other = last - one
            real = real + cos[one] * taps_cos[other] - sin[one] * taps_sin[other]
            imag = imag + cos[one] * taps_sin[other] + sin[one] * taps_cos[other]
        both = jnp.concatenate([real, imag])
        reach = block if last == count - 1 else 2 * block
        back = jnp.einsum("ft,fc->tc", table[:, :reach], both, precision=lax.Precision.HIGH) / block
        here = back[:block]
        outputs.append(here if spill is None else here + spill)
        spill = back[block:]
    return outputs[0] if count == 1 else jnp.concatenate(outputs)


def halves(value):
    high = value.astype(jnp.bfloat16)
    return high, (value - high.astype(jnp.float32)).astype(jnp.bfloat16)


def split_tables(block):
    table = tables(block)[:, :block]
    out = []
    for part in (table, table.T / np.float32(block)):
        high = part.astype(jnp.bfloat16)
        out += [high, (part - high.astype(np.float32)).astype(jnp.bfloat16)]
    return out


def wide_dot(high, low, value, dims):
    dot = functools.partial(lax.dot_general, dimension_numbers=(dims, ((), ())), preferred_element_type=jnp.float32)
    upper, lower = halves(value)
    free = 1 - dims[1][0]
    width = value.shape[free]
    both = dot(high, jnp.concatenate([upper, lower], axis=free))
    return both[:, :width] + both[:, width:] + dot(low, upper)


def filter_kernel(high_ref, low_ref, taps_ref, out_ref):
    out_ref[...] = wide_dot(high_ref[...], low_ref[...], taps_ref[...], ((1,), (1,)))


def local_kernel(groups, seq, sub, t_ref, taps_ref, *refs):
    count = seq * len(groups)
    moved = count + 5
    sources, outs = refs[:moved], refs[moved : moved + 2]
    proj, gated, sems = refs[moved + 2 : moved + 5]
    held = refs[moved + 5 :]
    copies = [pltpu.make_async_copy(sources[i], held[i], sems.at[i]) for i in range(moved)]
    for copy in copies:
        copy.start()
    terms = held[:count]
    fore_high, fore_low, spectrum_ref, back_high, back_low = held[count:]
    t = t_ref[0]
    length = gated.shape[0]
    shard = length // seq
    tensor = shard // sub

    def place(slot, source, lead):
        return pl.ds(pl.multiple_of(lead + source * shard + (t ^ slot) * sub, 8), sub)

    proj[:, :8] = jnp.zeros((proj.shape[0], 8, proj.shape[2]), jnp.float32)
    for group, slots in enumerate(groups):
        mine = terms[group * seq : (group + 1) * seq]
        for copy in copies[group * seq : (group + 1) * seq]:
            copy.wait()
        for position, slot in enumerate(slots):
            for source in range(seq):
                rows = pl.ds((position * seq + source) * sub, sub)
                total = mine[0][:, rows]
                for term in mine[1:]:
                    total = total + term[:, rows].astype(jnp.float32)
                proj[:, place(slot, source, 8)] = total

    def mixed(stream):
        total = taps_ref[stream, 0:1] * proj[stream, pl.ds(8, length)]
        for offset in range(1, taps_ref.shape[1]):
            total = total + taps_ref[stream, offset : offset + 1] * proj[stream, pl.ds(8 - offset, length)]
        return total

    signal = mixed(1) * mixed(2)
    for copy in copies[count : count + 3]:
        copy.wait()
    both = wide_dot(fore_high[...], fore_low[...], signal, ((1,), (0,)))
    cos, sin = both[:length], both[length:]
    taps_cos, taps_sin = spectrum_ref[:length], spectrum_ref[length:]
    both = jnp.concatenate([cos * taps_cos - sin * taps_sin, cos * taps_sin + sin * taps_cos])
    for copy in copies[count + 3 :]:
        copy.wait()
    gated[...] = mixed(0) * wide_dot(back_high[...], back_low[...], both, ((1,), (0,)))
    for slot in range(tensor):
        out = outs[slot // (tensor // 2)]
        for source in range(seq):
            row = ((slot % (tensor // 2)) * seq + source) * sub
            out[row : row + sub] = gated[place(slot, source, 0)].astype(jnp.bfloat16)


def local_stage(groups, terms, taps, long_filter, t, seq, sub):
    own, length = long_filter.shape
    wide = split_tables(length)
    vmem = pl.BlockSpec(memory_space=pltpu.VMEM)
    make_spectrum = pl.pallas_call(
        filter_kernel,
        out_shape=jax.ShapeDtypeStruct((2 * length, own), jnp.float32),
        in_specs=[vmem] * 3,
        out_specs=vmem,
        name="filter_spectrum",
        cost_estimate=pl.CostEstimate(flops=12 * length * length * own, bytes_accessed=4 * length * length, transcendentals=0),
    )
    spectrum = make_spectrum(*wide[:2], long_filter)
    flat = [term for group in terms for term in group]
    lines = length // 2
    moved = [*flat, *wide[:2], spectrum, *wide[2:]]
    return pl.pallas_call(
        functools.partial(local_kernel, groups, seq, sub),
        out_shape=[jax.ShapeDtypeStruct((lines, own), jnp.bfloat16)] * 2,
        in_specs=[pl.BlockSpec(memory_space=pltpu.SMEM), vmem] + [pl.BlockSpec(memory_space=pl.ANY)] * len(moved),
        out_specs=[vmem] * 2,
        scratch_shapes=[
            pltpu.VMEM((3, length + 8, own), jnp.float32),
            pltpu.VMEM((length, own), jnp.float32),
            pltpu.SemaphoreType.DMA((len(moved),)),
            *(pltpu.VMEM(part.shape, part.dtype) for part in moved),
        ],
        name="filters",
        cost_estimate=pl.CostEstimate(flops=24 * length * length * own, bytes_accessed=8 * length * length, transcendentals=0),
    )(t.reshape(1).astype(jnp.int32), taps, *moved)


def plain_stage(terms, taps, long_filter, t, seq, sub):
    streams, _, own = terms[0][0].shape
    length = long_filter.shape[1]
    tensor = length // (seq * sub)
    sums = []
    for group in terms:
        total = group[0]
        for term in group[1:]:
            total = total + term.astype(jnp.float32)
        sums.append(total)
    slots = range(tensor)
    projected = jnp.concatenate(sums, axis=1).reshape(streams, tensor, seq, sub, own)
    projected = jnp.stack([lax.dynamic_index_in_dim(projected, t ^ slot, 1, keepdims=False) for slot in slots], axis=2)
    projected = projected.reshape(streams, length, own)
    reach = taps.shape[1] - 1
    padded = jnp.pad(projected, ((0, 0), (reach, 0), (0, 0)))
    mixed = 0.0
    for offset in range(reach + 1):
        mixed = mixed + taps[:, offset, None] * padded[:, reach - offset : reach - offset + length]
    query, key, value = mixed
    conv = causal_convolution(key * value, long_filter)
    gated = (query * conv).astype(jnp.bfloat16).reshape(seq, tensor, sub, own)
    gated = [lax.dynamic_index_in_dim(gated, t ^ slot, 1, keepdims=False) for slot in slots]
    return [rows.reshape(seq * sub, own) for rows in gated]


def shards(residual_in, norm_gain, in_weight, short_taps, long_filter, out_weight):
    seq, tensor = lax.axis_size("seq"), lax.axis_size("tensor")
    z, t = lax.axis_index("seq"), lax.axis_index("tensor")
    rows, width = residual_in.shape
    _, depth, channels = in_weight.shape
    model = width * tensor
    sub = rows // tensor
    own = channels // seq
    length = rows * seq
    slots = range(tensor)

    whole = exchange(residual_in.astype(jnp.bfloat16).reshape(tensor, sub, width), "tensor")

    def in_part(mask):
        return lax.dynamic_slice_in_dim(in_weight, (z ^ mask) * own, own, 2)

    out_parts = [lax.dynamic_slice_in_dim(out_weight, (z ^ mask) * own, own, 1) for mask in range(seq)]
    out_turned = jnp.concatenate(out_parts, axis=1)
    taps = lax.dynamic_slice_in_dim(short_taps, z * own, own, 2)
    whole = whole.transpose(1, 0, 2).reshape(sub, model).astype(jnp.float32)
    mean_sq = jnp.mean(whole * whole, axis=1, keepdims=True)
    normed = (whole * lax.rsqrt(mean_sq + EPSILON) * norm_gain).astype(jnp.bfloat16)
    normed = exchange(normed.reshape(sub, seq, depth).transpose(1, 0, 2), "seq")
    parts = spread(normed.reshape(seq * sub, depth), "tensor")
    groups = (tuple(slots[:1]), tuple(slots[1:]))
    terms = []
    for group in groups:
        terms.append(sum_over_seq(jnp.concatenate([parts[slot] for slot in group]), in_part))
    half = tensor // 2
    if own % 128 == 0 and length <= BLOCK and sub % 16 == 0:
        lower_gated, upper_gated = local_stage(groups, terms, taps, long_filter, t, seq, sub)
    else:
        gated = plain_stage(terms, taps, long_filter, t, seq, sub)
        lower_gated = jnp.concatenate(gated[:half])
        upper_gated = jnp.concatenate(gated[half:])

    lower = [1 << bit for bit in range(half.bit_length() - 1)]
    held = None
    for chosen, piece in ((slots[half:], upper_gated), (slots[:half], lower_gated)):
        got = [piece] + [hop(piece, "seq", mask) for mask in range(1, seq)]
        got = jnp.concatenate(got, axis=1)
        terms = {}
        for place, slot in enumerate(chosen):
            terms[slot] = jnp.einsum(
                "rc,nc->rn",
                got[place * seq * sub : (place + 1) * seq * sub],
                out_turned,
                preferred_element_type=jnp.float32,
            )
        terms = fold(terms, "tensor", lower)
        if held is None:
            held = hop(terms[half].astype(jnp.bfloat16), "tensor", half)
        else:
            held = (terms[0] + held.astype(jnp.float32)).astype(jnp.bfloat16)
    back = exchange(held.reshape(seq, sub, depth), "seq")
    back = back.transpose(1, 0, 2).reshape(sub, tensor, width).transpose(1, 0, 2)
    summed = exchange(back, "tensor").reshape(rows, width)
    return residual_in + summed.astype(jnp.float32)


def solution(mesh):
    return jax.shard_map(
        shards,
        mesh=mesh,
        in_specs=(
            P(("groups", "seq"), "tensor"),
            P(),
            P(None, "seq", "tensor"),
            P(None, None, "tensor"),
            P(("tensor", "seq"), None),
            P("seq", "tensor"),
        ),
        out_specs=P(("groups", "seq"), "tensor"),
        check_vma=False,
    )
```

```python
import functools

import jax
import jax.numpy as jnp
import numpy as np
from jax import lax
from jax.experimental import pallas as pl
from jax.experimental.pallas import tpu as pltpu
from jax.sharding import PartitionSpec as P


EPSILON = 1e-05
BLOCK = 512


def pick(stacked, index):
    return lax.dynamic_index_in_dim(stacked, index, 0, keepdims=False)


def hop(value, axis, mask):
    count = lax.axis_size(axis)
    return lax.ppermute(value, axis, [(a, a ^ mask) for a in range(count)])


def exchange(blocks, axis):
    me = lax.axis_index(axis)
    count = lax.axis_size(axis)
    got = [pick(blocks, me)]
    got += [hop(pick(blocks, me ^ mask), axis, mask) for mask in range(1, count)]
    got = jnp.stack(got)
    return jnp.stack([pick(got, me ^ source) for source in range(count)])


def spread(value, axis):
    parts = {0: value}
    mask = lax.axis_size(axis) // 2
    while mask:
        parts.update({slot ^ mask: hop(part, axis, mask) for slot, part in parts.items()})
        mask //= 2
    return parts


def fold(parts, axis, masks):
    parts = dict(parts)
    for mask in masks:
        for slot in sorted(parts, reverse=True):
            if slot & mask:
                came = hop(parts.pop(slot).astype(jnp.bfloat16), axis, mask)
                parts[slot ^ mask] = parts[slot ^ mask] + came.astype(jnp.float32)
    return parts


def sum_over_seq(rows, weight_of):
    count = lax.axis_size("seq")
    narrow = weight_of(0).shape[2] % 128 != 0

    def product(mask):
        form = "rd,sdc->scr" if narrow else "rd,sdc->src"
        return jnp.einsum(form, rows, weight_of(mask), preferred_element_type=jnp.float32)

    low = jnp.bfloat16
    if count != 4:
        sent = {mask: product(mask).astype(low) for mask in range(1, count)}
        came = [hop(sent[mask], "seq", mask) for mask in sent]
    else:
        crossing = product(3).astype(low)
        relayed = lax.ppermute(crossing, "seq", [(0, 1), (3, 2)])
        middle = lax.ppermute(crossing, "seq", [(1, 2), (2, 1)])
        skipped = lax.ppermute(product(2).astype(low), "seq", [(0, 2), (3, 1)])
        near = hop(product(1).astype(low), "seq", 1)
        rows, relayed = lax.optimization_barrier((rows, relayed))
        merged = (product(2) + relayed.astype(jnp.float32)).astype(low)
        merged = lax.ppermute(merged, "seq", [(1, 3), (2, 0)])
        came = [near, middle, skipped, merged]
    if narrow:
        return [term.transpose(0, 2, 1) for term in [product(0)] + came]
    return [product(0)] + came


def tables(block):
    odd = 2 * np.arange(block)[:, None] + 1
    theta = (odd * np.arange(2 * block)[None, :] % (4 * block)) * (np.pi / (2 * block))
    return np.concatenate([np.cos(theta), np.sin(theta)]).astype(np.float32)


def causal_convolution(signal, taps):
    length, channels = signal.shape
    block = min(length, BLOCK)
    count = length // block
    table = jnp.asarray(tables(block))
    forward = table[:, :block]
    taps_all = jnp.einsum("ft,ckt->kfc", forward, taps.reshape(channels, count, block), precision=lax.Precision.HIGH)
    taps_cos, taps_sin = taps_all[:, :block], taps_all[:, block:]
    both = jnp.stack(
        [
            jnp.einsum("ft,tc->fc", forward, signal[one * block : (one + 1) * block], precision=lax.Precision.HIGH)
            for one in range(count)
        ]
    )
    cos, sin = both[:, :block], both[:, block:]
    outputs = []
    spill = None
    for last in range(count):
        real = imag = 0.0
        for one in range(last + 1):
            other = last - one
            real = real + cos[one] * taps_cos[other] - sin[one] * taps_sin[other]
            imag = imag + cos[one] * taps_sin[other] + sin[one] * taps_cos[other]
        both = jnp.concatenate([real, imag])
        reach = block if last == count - 1 else 2 * block
        back = jnp.einsum("ft,fc->tc", table[:, :reach], both, precision=lax.Precision.HIGH) / block
        here = back[:block]
        outputs.append(here if spill is None else here + spill)
        spill = back[block:]
    return outputs[0] if count == 1 else jnp.concatenate(outputs)


def halves(value):
    high = value.astype(jnp.bfloat16)
    return high, (value - high.astype(jnp.float32)).astype(jnp.bfloat16)


def split_tables(block):
    table = tables(block)[:, :block]
    out = []
    for part in (table, table.T / np.float32(block)):
        high = part.astype(jnp.bfloat16)
        out += [high, (part - high.astype(np.float32)).astype(jnp.bfloat16)]
    return out


def wide_dot(high, low, value, dims):
    dot = functools.partial(lax.dot_general, dimension_numbers=(dims, ((), ())), preferred_element_type=jnp.float32)
    upper, lower = halves(value)
    free = 1 - dims[1][0]
    width = value.shape[free]
    both = dot(high, jnp.concatenate([upper, lower], axis=free))
    return both[:, :width] + both[:, width:] + dot(low, upper)


def filter_kernel(high_ref, low_ref, taps_ref, out_ref):
    out_ref[...] = wide_dot(high_ref[...], low_ref[...], taps_ref[...], ((1,), (1,)))


def local_kernel(groups, each, seq, sub, t_ref, taps_ref, *refs):
    count = each * len(groups)
    moved = count + 5
    sources, outs = refs[:moved], refs[moved : moved + 2]
    proj, gated, sems = refs[moved + 2 : moved + 5]
    held = refs[moved + 5 :]
    copies = [pltpu.make_async_copy(sources[i], held[i], sems.at[i]) for i in range(moved)]
    for copy in copies:
        copy.start()
    terms = held[:count]
    fore_high, fore_low, spectrum_ref, back_high, back_low = held[count:]
    t = t_ref[0]
    length = gated.shape[0]
    shard = length // seq
    tensor = shard // sub

    def place(slot, source, lead):
        return pl.ds(pl.multiple_of(lead + source * shard + (t ^ slot) * sub, 8), sub)

    proj[:, :8] = jnp.zeros((proj.shape[0], 8, proj.shape[2]), jnp.float32)
    for group, slots in enumerate(groups):
        mine = terms[group * each : (group + 1) * each]
        for copy in copies[group * each : (group + 1) * each]:
            copy.wait()
        for position, slot in enumerate(slots):
            for source in range(seq):
                rows = pl.ds((position * seq + source) * sub, sub)
                total = mine[0][:, rows]
                for term in mine[1:]:
                    total = total + term[:, rows].astype(jnp.float32)
                proj[:, place(slot, source, 8)] = total

    def mixed(stream):
        total = taps_ref[stream, 0:1] * proj[stream, pl.ds(8, length)]
        for offset in range(1, taps_ref.shape[1]):
            total = total + taps_ref[stream, offset : offset + 1] * proj[stream, pl.ds(8 - offset, length)]
        return total

    signal = mixed(1) * mixed(2)
    for copy in copies[count : count + 3]:
        copy.wait()
    both = wide_dot(fore_high[...], fore_low[...], signal, ((1,), (0,)))
    cos, sin = both[:length], both[length:]
    taps_cos, taps_sin = spectrum_ref[:length], spectrum_ref[length:]
    both = jnp.concatenate([cos * taps_cos - sin * taps_sin, cos * taps_sin + sin * taps_cos])
    for copy in copies[count + 3 :]:
        copy.wait()
    gated[...] = mixed(0) * wide_dot(back_high[...], back_low[...], both, ((1,), (0,)))
    for slot in range(tensor):
        out = outs[slot // (tensor // 2)]
        for source in range(seq):
            row = ((slot % (tensor // 2)) * seq + source) * sub
            out[row : row + sub] = gated[place(slot, source, 0)].astype(jnp.bfloat16)


def local_stage(groups, terms, taps, long_filter, t, seq, sub):
    own, length = long_filter.shape
    wide = split_tables(length)
    vmem = pl.BlockSpec(memory_space=pltpu.VMEM)
    make_spectrum = pl.pallas_call(
        filter_kernel,
        out_shape=jax.ShapeDtypeStruct((2 * length, own), jnp.float32),
        in_specs=[vmem] * 3,
        out_specs=vmem,
        name="filter_spectrum",
        cost_estimate=pl.CostEstimate(flops=12 * length * length * own, bytes_accessed=4 * length * length, transcendentals=0),
    )
    spectrum = make_spectrum(*wide[:2], long_filter)
    flat = [term for group in terms for term in group]
    lines = length // 2
    moved = [*flat, *wide[:2], spectrum, *wide[2:]]
    return pl.pallas_call(
        functools.partial(local_kernel, groups, len(terms[0]), seq, sub),
        out_shape=[jax.ShapeDtypeStruct((lines, own), jnp.bfloat16)] * 2,
        in_specs=[pl.BlockSpec(memory_space=pltpu.SMEM), vmem] + [pl.BlockSpec(memory_space=pl.ANY)] * len(moved),
        out_specs=[vmem] * 2,
        scratch_shapes=[
            pltpu.VMEM((3, length + 8, own), jnp.float32),
            pltpu.VMEM((length, own), jnp.float32),
            pltpu.SemaphoreType.DMA((len(moved),)),
            *(pltpu.VMEM(part.shape, part.dtype) for part in moved),
        ],
        name="filters",
        cost_estimate=pl.CostEstimate(flops=24 * length * length * own, bytes_accessed=8 * length * length, transcendentals=0),
    )(t.reshape(1).astype(jnp.int32), taps, *moved)


def plain_stage(terms, taps, long_filter, t, seq, sub):
    streams, _, own = terms[0][0].shape
    length = long_filter.shape[1]
    tensor = length // (seq * sub)
    sums = []
    for group in terms:
        total = group[0]
        for term in group[1:]:
            total = total + term.astype(jnp.float32)
        sums.append(total)
    slots = range(tensor)
    projected = jnp.concatenate(sums, axis=1).reshape(streams, tensor, seq, sub, own)
    projected = jnp.stack([lax.dynamic_index_in_dim(projected, t ^ slot, 1, keepdims=False) for slot in slots], axis=2)
    projected = projected.reshape(streams, length, own)
    reach = taps.shape[1] - 1
    padded = jnp.pad(projected, ((0, 0), (reach, 0), (0, 0)))
    mixed = 0.0
    for offset in range(reach + 1):
        mixed = mixed + taps[:, offset, None] * padded[:, reach - offset : reach - offset + length]
    query, key, value = mixed
    conv = causal_convolution(key * value, long_filter)
    gated = (query * conv).astype(jnp.bfloat16).reshape(seq, tensor, sub, own)
    gated = [lax.dynamic_index_in_dim(gated, t ^ slot, 1, keepdims=False) for slot in slots]
    return [rows.reshape(seq * sub, own) for rows in gated]


def shards(residual_in, norm_gain, in_weight, short_taps, long_filter, out_weight):
    seq, tensor = lax.axis_size("seq"), lax.axis_size("tensor")
    z, t = lax.axis_index("seq"), lax.axis_index("tensor")
    rows, width = residual_in.shape
    _, depth, channels = in_weight.shape
    model = width * tensor
    sub = rows // tensor
    own = channels // seq
    length = rows * seq
    slots = range(tensor)

    whole = exchange(residual_in.astype(jnp.bfloat16).reshape(tensor, sub, width), "tensor")

    def in_part(mask):
        return lax.dynamic_slice_in_dim(in_weight, (z ^ mask) * own, own, 2)

    out_parts = [lax.dynamic_slice_in_dim(out_weight, (z ^ mask) * own, own, 1) for mask in range(seq)]
    out_turned = jnp.concatenate(out_parts, axis=1)
    taps = lax.dynamic_slice_in_dim(short_taps, z * own, own, 2)
    whole = whole.transpose(1, 0, 2).reshape(sub, model).astype(jnp.float32)
    mean_sq = jnp.mean(whole * whole, axis=1, keepdims=True)
    normed = (whole * lax.rsqrt(mean_sq + EPSILON) * norm_gain).astype(jnp.bfloat16)
    normed = exchange(normed.reshape(sub, seq, depth).transpose(1, 0, 2), "seq")
    parts = spread(normed.reshape(seq * sub, depth), "tensor")
    groups = (tuple(slots[:1]), tuple(slots[1:]))
    terms = []
    for group in groups:
        terms.append(sum_over_seq(jnp.concatenate([parts[slot] for slot in group]), in_part))
    half = tensor // 2
    if own % 128 == 0 and length <= BLOCK and sub % 16 == 0:
        lower_gated, upper_gated = local_stage(groups, terms, taps, long_filter, t, seq, sub)
    else:
        gated = plain_stage(terms, taps, long_filter, t, seq, sub)
        lower_gated = jnp.concatenate(gated[:half])
        upper_gated = jnp.concatenate(gated[half:])

    lower = [1 << bit for bit in range(half.bit_length() - 1)]
    held = None
    for chosen, piece in ((slots[half:], upper_gated), (slots[:half], lower_gated)):
        got = [piece] + [hop(piece, "seq", mask) for mask in range(1, seq)]
        got = jnp.concatenate(got, axis=1)
        terms = {}
        for place, slot in enumerate(chosen):
            terms[slot] = jnp.einsum(
                "rc,nc->rn",
                got[place * seq * sub : (place + 1) * seq * sub],
                out_turned,
                preferred_element_type=jnp.float32,
            )
        terms = fold(terms, "tensor", lower)
        if held is None:
            held = hop(terms[half].astype(jnp.bfloat16), "tensor", half)
        else:
            held = (terms[0] + held.astype(jnp.float32)).astype(jnp.bfloat16)
    back = exchange(held.reshape(seq, sub, depth), "seq")
    back = back.transpose(1, 0, 2).reshape(sub, tensor, width).transpose(1, 0, 2)
    summed = exchange(back, "tensor").reshape(rows, width)
    return residual_in + summed.astype(jnp.float32)


def solution(mesh):
    return jax.shard_map(
        shards,
        mesh=mesh,
        in_specs=(
            P(("groups", "seq"), "tensor"),
            P(),
            P(None, "seq", "tensor"),
            P(None, None, "tensor"),
            P(("tensor", "seq"), None),
            P("seq", "tensor"),
        ),
        out_specs=P(("groups", "seq"), "tensor"),
        check_vma=False,
    )
```

```python
import functools

import jax
import jax.numpy as jnp
import numpy as np
from jax import lax
from jax.experimental import pallas as pl
from jax.experimental.pallas import tpu as pltpu
from jax.sharding import PartitionSpec as P


EPSILON = 1e-05
BLOCK = 512


def pick(stacked, index):
    return lax.dynamic_index_in_dim(stacked, index, 0, keepdims=False)


def hop(value, axis, mask):
    count = lax.axis_size(axis)
    return lax.ppermute(value, axis, [(a, a ^ mask) for a in range(count)])


def exchange(blocks, axis):
    me = lax.axis_index(axis)
    count = lax.axis_size(axis)
    got = [pick(blocks, me)]
    got += [hop(pick(blocks, me ^ mask), axis, mask) for mask in range(1, count)]
    got = jnp.stack(got)
    return jnp.stack([pick(got, me ^ source) for source in range(count)])


def spread(value, axis):
    parts = {0: value}
    mask = lax.axis_size(axis) // 2
    while mask:
        for slot, part in list(parts.items()):
            parts[slot ^ mask] = hop(part, axis, mask)
        mask //= 2
    return parts


def fold(parts, axis, masks):
    parts = dict(parts)
    for mask in masks:
        for slot in sorted(parts, reverse=True):
            if slot & mask:
                came = hop(parts.pop(slot).astype(jnp.bfloat16), axis, mask)
                parts[slot ^ mask] = parts[slot ^ mask] + came.astype(jnp.float32)
    return parts


def sum_over_seq(rows, weight_of):
    count = lax.axis_size("seq")
    narrow = weight_of(0).shape[2] % 128 != 0

    def product(mask):
        form = "rd,sdc->scr" if narrow else "rd,sdc->src"
        return jnp.einsum(form, rows, weight_of(mask), preferred_element_type=jnp.float32)

    low = jnp.bfloat16
    if count != 4:
        sent = {mask: product(mask).astype(low) for mask in range(1, count)}
        came = [hop(sent[mask], "seq", mask) for mask in sent]
    else:
        z = lax.axis_index("seq")
        end = (z == 0) | (z == 3)
        first = hop(product(jnp.where(end, 3, 1)).astype(low), "seq", 1)
        second = product(jnp.where(end, 1, 3)).astype(low)
        middle = lax.ppermute(second, "seq", [(1, 2), (2, 1)])
        near = lax.ppermute(second, "seq", [(0, 1), (3, 2)])
        rows, first = lax.optimization_barrier((rows, first))
        relayed = jnp.where(end, 0.0, first.astype(jnp.float32))
        last = hop((product(2) + relayed).astype(low), "seq", 2)
        total = product(0) + jnp.where(end, first.astype(jnp.float32), 0.0)
        total = total + middle.astype(jnp.float32) + near.astype(jnp.float32)
        return [total, last]
    if narrow:
        return [term.transpose(0, 2, 1) for term in [product(0)] + came]
    return [product(0)] + came


def tables(block):
    odd = 2 * np.arange(block)[:, None] + 1
    theta = (odd * np.arange(2 * block)[None, :] % (4 * block)) * (np.pi / (2 * block))
    return np.concatenate([np.cos(theta), np.sin(theta)]).astype(np.float32)


def causal_convolution(signal, taps):
    length, channels = signal.shape
    block = min(length, BLOCK)
    count = length // block
    table = jnp.asarray(tables(block))
    forward = table[:, :block]
    taps_all = jnp.einsum("ft,ckt->kfc", forward, taps.reshape(channels, count, block), precision=lax.Precision.HIGH)
    taps_cos, taps_sin = taps_all[:, :block], taps_all[:, block:]
    both = jnp.stack(
        [
            jnp.einsum("ft,tc->fc", forward, signal[one * block : (one + 1) * block], precision=lax.Precision.HIGH)
            for one in range(count)
        ]
    )
    cos, sin = both[:, :block], both[:, block:]
    outputs = []
    spill = None
    for last in range(count):
        real = imag = 0.0
        for one in range(last + 1):
            other = last - one
            real = real + cos[one] * taps_cos[other] - sin[one] * taps_sin[other]
            imag = imag + cos[one] * taps_sin[other] + sin[one] * taps_cos[other]
        both = jnp.concatenate([real, imag])
        reach = block if last == count - 1 else 2 * block
        back = jnp.einsum("ft,fc->tc", table[:, :reach], both, precision=lax.Precision.HIGH) / block
        here = back[:block]
        outputs.append(here if spill is None else here + spill)
        spill = back[block:]
    return outputs[0] if count == 1 else jnp.concatenate(outputs)


def halves(value):
    high = value.astype(jnp.bfloat16)
    return high, (value - high.astype(jnp.float32)).astype(jnp.bfloat16)


def split_tables(block):
    table = tables(block)[:, :block]
    out = []
    for part in (table, table.T / np.float32(block)):
        high = part.astype(jnp.bfloat16)
        out += [high, (part - high.astype(np.float32)).astype(jnp.bfloat16)]
    return out


def wide_dot(high, low, value, dims):
    dot = functools.partial(lax.dot_general, dimension_numbers=(dims, ((), ())), preferred_element_type=jnp.float32)
    upper, lower = halves(value)
    free = 1 - dims[1][0]
    width = value.shape[free]
    both = dot(high, jnp.concatenate([upper, lower], axis=free))
    return both[:, :width] + both[:, width:] + dot(low, upper)


def filter_kernel(high_ref, low_ref, taps_ref, out_ref):
    out_ref[...] = wide_dot(high_ref[...], low_ref[...], taps_ref[...], ((1,), (1,)))


def local_kernel(groups, each, seq, sub, t_ref, taps_ref, *refs):
    count = each * len(groups)
    moved = count + 5
    sources, outs = refs[:moved], refs[moved : moved + 2]
    proj, gated, sems = refs[moved + 2 : moved + 5]
    held = refs[moved + 5 :]
    copies = [pltpu.make_async_copy(sources[i], held[i], sems.at[i]) for i in range(moved)]
    for copy in copies:
        copy.start()
    terms = held[:count]
    fore_high, fore_low, spectrum_ref, back_high, back_low = held[count:]
    t = t_ref[0]
    length = gated.shape[0]
    shard = length // seq
    tensor = shard // sub

    def place(slot, source, lead):
        return pl.ds(pl.multiple_of(lead + source * shard + (t ^ slot) * sub, 8), sub)

    proj[:, :8] = jnp.zeros((proj.shape[0], 8, proj.shape[2]), jnp.float32)
    for group, slots in enumerate(groups):
        mine = terms[group * each : (group + 1) * each]
        for copy in copies[group * each : (group + 1) * each]:
            copy.wait()
        for position, slot in enumerate(slots):
            for source in range(seq):
                rows = pl.ds((position * seq + source) * sub, sub)
                total = mine[0][:, rows]
                for term in mine[1:]:
                    total = total + term[:, rows].astype(jnp.float32)
                proj[:, place(slot, source, 8)] = total

    def mixed(stream):
        total = taps_ref[stream, 0:1] * proj[stream, pl.ds(8, length)]
        for offset in range(1, taps_ref.shape[1]):
            total = total + taps_ref[stream, offset : offset + 1] * proj[stream, pl.ds(8 - offset, length)]
        return total

    signal = mixed(1) * mixed(2)
    for copy in copies[count : count + 3]:
        copy.wait()
    both = wide_dot(fore_high[...], fore_low[...], signal, ((1,), (0,)))
    cos, sin = both[:length], both[length:]
    taps_cos, taps_sin = spectrum_ref[:length], spectrum_ref[length:]
    both = jnp.concatenate([cos * taps_cos - sin * taps_sin, cos * taps_sin + sin * taps_cos])
    for copy in copies[count + 3 :]:
        copy.wait()
    gated[...] = mixed(0) * wide_dot(back_high[...], back_low[...], both, ((1,), (0,)))
    for slot in range(tensor):
        out = outs[slot // (tensor // 2)]
        for source in range(seq):
            row = ((slot % (tensor // 2)) * seq + source) * sub
            out[row : row + sub] = gated[place(slot, source, 0)].astype(jnp.bfloat16)


def local_stage(groups, terms, taps, long_filter, t, seq, sub):
    own, length = long_filter.shape
    wide = split_tables(length)
    vmem = pl.BlockSpec(memory_space=pltpu.VMEM)
    make_spectrum = pl.pallas_call(
        filter_kernel,
        out_shape=jax.ShapeDtypeStruct((2 * length, own), jnp.float32),
        in_specs=[vmem] * 3,
        out_specs=vmem,
        name="filter_spectrum",
        cost_estimate=pl.CostEstimate(flops=12 * length * length * own, bytes_accessed=4 * length * length, transcendentals=0),
    )
    spectrum = make_spectrum(*wide[:2], long_filter)
    flat = [term for group in terms for term in group]
    lines = length // 2
    moved = [*flat, *wide[:2], spectrum, *wide[2:]]
    return pl.pallas_call(
        functools.partial(local_kernel, groups, len(terms[0]), seq, sub),
        out_shape=[jax.ShapeDtypeStruct((lines, own), jnp.bfloat16)] * 2,
        in_specs=[pl.BlockSpec(memory_space=pltpu.SMEM), vmem] + [pl.BlockSpec(memory_space=pl.ANY)] * len(moved),
        out_specs=[vmem] * 2,
        scratch_shapes=[
            pltpu.VMEM((3, length + 8, own), jnp.float32),
            pltpu.VMEM((length, own), jnp.float32),
            pltpu.SemaphoreType.DMA((len(moved),)),
            *(pltpu.VMEM(part.shape, part.dtype) for part in moved),
        ],
        name="filters",
        cost_estimate=pl.CostEstimate(flops=24 * length * length * own, bytes_accessed=8 * length * length, transcendentals=0),
    )(t.reshape(1).astype(jnp.int32), taps, *moved)


def plain_stage(terms, taps, long_filter, t, seq, sub):
    streams, _, own = terms[0][0].shape
    length = long_filter.shape[1]
    tensor = length // (seq * sub)
    sums = []
    for group in terms:
        total = group[0]
        for term in group[1:]:
            total = total + term.astype(jnp.float32)
        sums.append(total)
    slots = range(tensor)
    projected = jnp.concatenate(sums, axis=1).reshape(streams, tensor, seq, sub, own)
    projected = jnp.stack([lax.dynamic_index_in_dim(projected, t ^ slot, 1, keepdims=False) for slot in slots], axis=2)
    projected = projected.reshape(streams, length, own)
    reach = taps.shape[1] - 1
    padded = jnp.pad(projected, ((0, 0), (reach, 0), (0, 0)))
    mixed = 0.0
    for offset in range(reach + 1):
        mixed = mixed + taps[:, offset, None] * padded[:, reach - offset : reach - offset + length]
    query, key, value = mixed
    conv = causal_convolution(key * value, long_filter)
    gated = (query * conv).astype(jnp.bfloat16).reshape(seq, tensor, sub, own)
    gated = [lax.dynamic_index_in_dim(gated, t ^ slot, 1, keepdims=False) for slot in slots]
    return [rows.reshape(seq * sub, own) for rows in gated]


def shards(residual_in, norm_gain, in_weight, short_taps, long_filter, out_weight):
    seq, tensor = lax.axis_size("seq"), lax.axis_size("tensor")
    z, t = lax.axis_index("seq"), lax.axis_index("tensor")
    rows, width = residual_in.shape
    _, depth, channels = in_weight.shape
    model = width * tensor
    sub = rows // tensor
    own = channels // seq
    length = rows * seq
    slots = range(tensor)

    whole = exchange(residual_in.astype(jnp.bfloat16).reshape(tensor, sub, width), "tensor")

    def in_part(mask):
        return lax.dynamic_slice_in_dim(in_weight, (z ^ mask) * own, own, 2)

    out_parts = [lax.dynamic_slice_in_dim(out_weight, (z ^ mask) * own, own, 1) for mask in range(seq)]
    out_turned = jnp.concatenate(out_parts, axis=1)
    taps = lax.dynamic_slice_in_dim(short_taps, z * own, own, 2)
    whole = whole.transpose(1, 0, 2).reshape(sub, model).astype(jnp.float32)
    mean_sq = jnp.mean(whole * whole, axis=1, keepdims=True)
    normed = (whole * lax.rsqrt(mean_sq + EPSILON) * norm_gain).astype(jnp.bfloat16)
    normed = exchange(normed.reshape(sub, seq, depth).transpose(1, 0, 2), "seq")
    parts = spread(normed.reshape(seq * sub, depth), "tensor")
    groups = (tuple(slots[:2]), tuple(slots[2:]))
    terms = []
    for group in groups:
        terms.append(sum_over_seq(jnp.concatenate([parts[slot] for slot in group]), in_part))
    half = tensor // 2
    if own % 128 == 0 and length <= BLOCK and sub % 16 == 0:
        lower_gated, upper_gated = local_stage(groups, terms, taps, long_filter, t, seq, sub)
    else:
        gated = plain_stage(terms, taps, long_filter, t, seq, sub)
        lower_gated = jnp.concatenate(gated[:half])
        upper_gated = jnp.concatenate(gated[half:])

    lower = [1 << bit for bit in range(half.bit_length() - 1)]
    held = None
    for chosen, piece in ((slots[half:], upper_gated), (slots[:half], lower_gated)):
        got = [piece] + [hop(piece, "seq", mask) for mask in range(1, seq)]
        got = jnp.concatenate(got, axis=1)
        terms = {}
        for place, slot in enumerate(chosen):
            terms[slot] = jnp.einsum(
                "rc,nc->rn",
                got[place * seq * sub : (place + 1) * seq * sub],
                out_turned,
                preferred_element_type=jnp.float32,
            )
        terms = fold(terms, "tensor", lower)
        if held is None:
            held = hop(terms[half].astype(jnp.bfloat16), "tensor", half)
        else:
            held = (terms[0] + held.astype(jnp.float32)).astype(jnp.bfloat16)
    back = exchange(held.reshape(seq, sub, depth), "seq")
    back = back.transpose(1, 0, 2).reshape(sub, tensor, width).transpose(1, 0, 2)
    summed = exchange(back, "tensor").reshape(rows, width)
    return residual_in + summed.astype(jnp.float32)


def solution(mesh):
    return jax.shard_map(
        shards,
        mesh=mesh,
        in_specs=(
            P(("groups", "seq"), "tensor"),
            P(),
            P(None, "seq", "tensor"),
            P(None, None, "tensor"),
            P(("tensor", "seq"), None),
            P("seq", "tensor"),
        ),
        out_specs=P(("groups", "seq"), "tensor"),
        check_vma=False,
    )
```

```python
import functools

import jax
import jax.numpy as jnp
import numpy as np
from jax import lax
from jax.experimental import pallas as pl
from jax.experimental.pallas import tpu as pltpu
from jax.sharding import PartitionSpec as P


EPSILON = 1e-05
BLOCK = 512


def pick(stacked, index):
    return lax.dynamic_index_in_dim(stacked, index, 0, keepdims=False)


def hop(value, axis, mask):
    count = lax.axis_size(axis)
    return lax.ppermute(value, axis, [(a, a ^ mask) for a in range(count)])


def exchange(blocks, axis):
    me = lax.axis_index(axis)
    count = lax.axis_size(axis)
    got = [pick(blocks, me)]
    got += [hop(pick(blocks, me ^ mask), axis, mask) for mask in range(1, count)]
    got = jnp.stack(got)
    return jnp.stack([pick(got, me ^ source) for source in range(count)])


def spread(value, axis):
    parts = {0: value}
    mask = lax.axis_size(axis) // 2
    while mask:
        for slot, part in list(parts.items()):
            parts[slot ^ mask] = hop(part, axis, mask)
        mask //= 2
    return parts


def fold(parts, axis, masks):
    parts = dict(parts)
    for mask in masks:
        for slot in sorted(parts, reverse=True):
            if slot & mask:
                came = hop(parts.pop(slot).astype(jnp.bfloat16), axis, mask)
                parts[slot ^ mask] = parts[slot ^ mask] + came.astype(jnp.float32)
    return parts


def sum_over_seq(rows, weight_of):
    count = lax.axis_size("seq")
    narrow = weight_of(0).shape[2] % 128 != 0

    def product(mask):
        form = "rd,sdc->scr" if narrow else "rd,sdc->src"
        return jnp.einsum(form, rows, weight_of(mask), preferred_element_type=jnp.float32)

    sent = {mask: product(mask).astype(jnp.bfloat16) for mask in range(1, count)}
    terms = [product(0)] + [hop(sent[mask], "seq", mask) for mask in sent]
    return [term.transpose(0, 2, 1) for term in terms] if narrow else terms


def project_kernel(pieces, chunks, ready, finish, index_ref, *refs):
    rows_refs, weight_ref, refs = refs[:pieces], refs[pieces], refs[pieces + 1 :]
    refs, (held, sems) = refs[:-2], refs[-2:]
    own = held.shape[3]
    z = index_ref[0]
    end = (z == 0) | (z == 3)
    copies = []
    for place, chunk in enumerate(chunks(z, end)):
        lanes = pl.ds(pl.multiple_of(chunk * own, own), own)
        copies.append(pltpu.make_async_copy(weight_ref.at[:, :, lanes], held.at[place], sems.at[place]))
        copies[-1].start()
    for place, copy in enumerate(copies):
        copy.wait()
        for stream in range(held.shape[1]):
            for piece, rows_ref in enumerate(rows_refs):
                size = rows_ref.shape[0]
                product = jnp.dot(rows_ref[...], held[place, stream], preferred_element_type=jnp.float32)
                rows = pl.ds(piece * size, size)
                finish(refs, place, stream, rows, product, ready(refs, stream, rows, end))


def no_terms(refs, stream, rows, end):
    return None


def finish_first(refs, place, stream, rows, product, added):
    low = product.astype(jnp.bfloat16)
    refs[0][place, stream, rows] = low
    if place:
        refs[1][stream, rows] = low


def relayed_terms(refs, stream, rows, end):
    return jnp.where(end, 0.0, refs[0][0, stream, rows].astype(jnp.float32))


def own_terms(refs, stream, rows, end):
    came = refs[0]
    first = came[0, stream, rows].astype(jnp.float32)
    second = came[1, stream, rows].astype(jnp.float32)
    return jnp.where(end, first, second) + refs[1][stream, rows].astype(jnp.float32)


def finish_sum(refs, place, stream, rows, product, added):
    refs[-1][stream, rows] = (product + added).astype(refs[-1].dtype)


def first_chunks(z, end):
    return [z ^ jnp.where(end, 3, 1), z ^ jnp.where(end, 1, 3)]


def third_chunk(z, end):
    return [z ^ 2]


def own_chunk(z, end):
    return [z]


def project(pieces, weight, z, chunks, count, terms, outs, ready, finish):
    vmem = pl.BlockSpec(memory_space=pltpu.VMEM)
    streams, depth, channels = weight.shape
    own = channels // lax.axis_size("seq")
    rows = sum(piece.shape[0] for piece in pieces)
    return pl.pallas_call(
        functools.partial(project_kernel, len(pieces), chunks, ready, finish),
        out_shape=outs,
        in_specs=[pl.BlockSpec(memory_space=pltpu.SMEM)]
        + [vmem] * len(pieces)
        + [pl.BlockSpec(memory_space=pl.ANY)]
        + [vmem] * len(terms),
        out_specs=[vmem] * len(outs),
        scratch_shapes=[
            pltpu.VMEM((count, streams, depth, own), weight.dtype),
            pltpu.SemaphoreType.DMA((count,)),
        ],
        cost_estimate=pl.CostEstimate(
            flops=2 * rows * depth * streams * own * count,
            bytes_accessed=2 * depth * streams * own * count,
            transcendentals=0,
        ),
    )(z.reshape(1).astype(jnp.int32), *pieces, weight, *terms)


def relay_sum(pieces, weight):
    z = lax.axis_index("seq")
    streams, _, channels = weight.shape
    rows = sum(piece.shape[0] for piece in pieces)
    shape = (streams, rows, channels // 4)
    low = jax.ShapeDtypeStruct(shape, jnp.bfloat16)
    outs = [jax.ShapeDtypeStruct((2, *shape), jnp.bfloat16), low]
    both, second = project(pieces, weight, z, first_chunks, 2, [], outs, no_terms, finish_first)
    came = hop(both, "seq", 1)
    middle = lax.ppermute(second, "seq", [(1, 2), (2, 1)])
    (merged,) = project(pieces, weight, z, third_chunk, 1, [came], [low], relayed_terms, finish_sum)
    last = hop(merged, "seq", 2)
    outs = [jax.ShapeDtypeStruct(shape, jnp.float32)]
    (total,) = project(pieces, weight, z, own_chunk, 1, [came, middle], outs, own_terms, finish_sum)
    return [total, last]


def tables(block):
    odd = 2 * np.arange(block)[:, None] + 1
    theta = (odd * np.arange(2 * block)[None, :] % (4 * block)) * (np.pi / (2 * block))
    return np.concatenate([np.cos(theta), np.sin(theta)]).astype(np.float32)


def causal_convolution(signal, taps):
    length, channels = signal.shape
    block = min(length, BLOCK)
    count = length // block
    table = jnp.asarray(tables(block))
    forward = table[:, :block]
    taps_all = jnp.einsum("ft,ckt->kfc", forward, taps.reshape(channels, count, block), precision=lax.Precision.HIGH)
    taps_cos, taps_sin = taps_all[:, :block], taps_all[:, block:]
    both = jnp.stack(
        [
            jnp.einsum("ft,tc->fc", forward, signal[one * block : (one + 1) * block], precision=lax.Precision.HIGH)
            for one in range(count)
        ]
    )
    cos, sin = both[:, :block], both[:, block:]
    outputs = []
    spill = None
    for last in range(count):
        real = imag = 0.0
        for one in range(last + 1):
            other = last - one
            real = real + cos[one] * taps_cos[other] - sin[one] * taps_sin[other]
            imag = imag + cos[one] * taps_sin[other] + sin[one] * taps_cos[other]
        both = jnp.concatenate([real, imag])
        reach = block if last == count - 1 else 2 * block
        back = jnp.einsum("ft,fc->tc", table[:, :reach], both, precision=lax.Precision.HIGH) / block
        here = back[:block]
        outputs.append(here if spill is None else here + spill)
        spill = back[block:]
    return outputs[0] if count == 1 else jnp.concatenate(outputs)


def halves(value):
    high = value.astype(jnp.bfloat16)
    return high, (value - high.astype(jnp.float32)).astype(jnp.bfloat16)


def split_tables(block):
    table = tables(block)[:, :block]
    out = []
    for part in (table, table.T / np.float32(block)):
        high = part.astype(jnp.bfloat16)
        out += [high, (part - high.astype(np.float32)).astype(jnp.bfloat16)]
    return out


def wide_dot(high, low, value, dims):
    dot = functools.partial(lax.dot_general, dimension_numbers=(dims, ((), ())), preferred_element_type=jnp.float32)
    upper, lower = halves(value)
    free = 1 - dims[1][0]
    width = value.shape[free]
    both = dot(high, jnp.concatenate([upper, lower], axis=free))
    return both[:, :width] + both[:, width:] + dot(low, upper)


def filter_kernel(high_ref, low_ref, taps_ref, out_ref):
    out_ref[...] = wide_dot(high_ref[...], low_ref[...], taps_ref[...], ((1,), (1,)))


def local_kernel(groups, each, seq, sub, t_ref, taps_ref, *refs):
    count = each * len(groups)
    moved = count + 5
    sources, outs = refs[:moved], refs[moved : moved + 2]
    proj, gated, sems = refs[moved + 2 : moved + 5]
    held = refs[moved + 5 :]
    copies = [pltpu.make_async_copy(sources[i], held[i], sems.at[i]) for i in range(moved)]
    for copy in copies:
        copy.start()
    terms = held[:count]
    fore_high, fore_low, spectrum_ref, back_high, back_low = held[count:]
    t = t_ref[0]
    length = gated.shape[0]
    shard = length // seq
    tensor = shard // sub

    def place(slot, source, lead):
        return pl.ds(pl.multiple_of(lead + source * shard + (t ^ slot) * sub, 8), sub)

    proj[:, :8] = jnp.zeros((proj.shape[0], 8, proj.shape[2]), jnp.float32)
    for group, slots in enumerate(groups):
        mine = terms[group * each : (group + 1) * each]
        for copy in copies[group * each : (group + 1) * each]:
            copy.wait()
        for position, slot in enumerate(slots):
            for source in range(seq):
                rows = pl.ds((position * seq + source) * sub, sub)
                total = mine[0][:, rows]
                for term in mine[1:]:
                    total = total + term[:, rows].astype(jnp.float32)
                proj[:, place(slot, source, 8)] = total

    def mixed(stream):
        total = taps_ref[stream, 0:1] * proj[stream, pl.ds(8, length)]
        for offset in range(1, taps_ref.shape[1]):
            total = total + taps_ref[stream, offset : offset + 1] * proj[stream, pl.ds(8 - offset, length)]
        return total

    signal = mixed(1) * mixed(2)
    for copy in copies[count : count + 3]:
        copy.wait()
    both = wide_dot(fore_high[...], fore_low[...], signal, ((1,), (0,)))
    cos, sin = both[:length], both[length:]
    taps_cos, taps_sin = spectrum_ref[:length], spectrum_ref[length:]
    both = jnp.concatenate([cos * taps_cos - sin * taps_sin, cos * taps_sin + sin * taps_cos])
    for copy in copies[count + 3 :]:
        copy.wait()
    gated[...] = mixed(0) * wide_dot(back_high[...], back_low[...], both, ((1,), (0,)))
    for slot in range(tensor):
        out = outs[slot // (tensor // 2)]
        for source in range(seq):
            row = ((slot % (tensor // 2)) * seq + source) * sub
            out[row : row + sub] = gated[place(slot, source, 0)].astype(jnp.bfloat16)


def local_stage(groups, terms, taps, long_filter, t, seq, sub):
    own, length = long_filter.shape
    wide = split_tables(length)
    vmem = pl.BlockSpec(memory_space=pltpu.VMEM)
    make_spectrum = pl.pallas_call(
        filter_kernel,
        out_shape=jax.ShapeDtypeStruct((2 * length, own), jnp.float32),
        in_specs=[vmem] * 3,
        out_specs=vmem,
        name="filter_spectrum",
        cost_estimate=pl.CostEstimate(flops=12 * length * length * own, bytes_accessed=4 * length * length, transcendentals=0),
    )
    spectrum = make_spectrum(*wide[:2], long_filter)
    flat = [term for group in terms for term in group]
    lines = length // 2
    moved = [*flat, *wide[:2], spectrum, *wide[2:]]
    return pl.pallas_call(
        functools.partial(local_kernel, groups, len(terms[0]), seq, sub),
        out_shape=[jax.ShapeDtypeStruct((lines, own), jnp.bfloat16)] * 2,
        in_specs=[pl.BlockSpec(memory_space=pltpu.SMEM), vmem] + [pl.BlockSpec(memory_space=pl.ANY)] * len(moved),
        out_specs=[vmem] * 2,
        scratch_shapes=[
            pltpu.VMEM((3, length + 8, own), jnp.float32),
            pltpu.VMEM((length, own), jnp.float32),
            pltpu.SemaphoreType.DMA((len(moved),)),
            *(pltpu.VMEM(part.shape, part.dtype) for part in moved),
        ],
        name="filters",
        cost_estimate=pl.CostEstimate(flops=24 * length * length * own, bytes_accessed=8 * length * length, transcendentals=0),
    )(t.reshape(1).astype(jnp.int32), taps, *moved)


def plain_stage(terms, taps, long_filter, t, seq, sub):
    streams, _, own = terms[0][0].shape
    length = long_filter.shape[1]
    tensor = length // (seq * sub)
    sums = []
    for group in terms:
        total = group[0]
        for term in group[1:]:
            total = total + term.astype(jnp.float32)
        sums.append(total)
    slots = range(tensor)
    projected = jnp.concatenate(sums, axis=1).reshape(streams, tensor, seq, sub, own)
    projected = jnp.stack([lax.dynamic_index_in_dim(projected, t ^ slot, 1, keepdims=False) for slot in slots], axis=2)
    projected = projected.reshape(streams, length, own)
    reach = taps.shape[1] - 1
    padded = jnp.pad(projected, ((0, 0), (reach, 0), (0, 0)))
    mixed = 0.0
    for offset in range(reach + 1):
        mixed = mixed + taps[:, offset, None] * padded[:, reach - offset : reach - offset + length]
    query, key, value = mixed
    conv = causal_convolution(key * value, long_filter)
    gated = (query * conv).astype(jnp.bfloat16).reshape(seq, tensor, sub, own)
    gated = [lax.dynamic_index_in_dim(gated, t ^ slot, 1, keepdims=False) for slot in slots]
    return [rows.reshape(seq * sub, own) for rows in gated]


def shards(residual_in, norm_gain, in_weight, short_taps, long_filter, out_weight):
    seq, tensor = lax.axis_size("seq"), lax.axis_size("tensor")
    z, t = lax.axis_index("seq"), lax.axis_index("tensor")
    rows, width = residual_in.shape
    _, depth, channels = in_weight.shape
    model = width * tensor
    sub = rows // tensor
    own = channels // seq
    length = rows * seq
    slots = range(tensor)

    whole = exchange(residual_in.astype(jnp.bfloat16).reshape(tensor, sub, width), "tensor")

    def in_part(mask):
        return lax.dynamic_slice_in_dim(in_weight, (z ^ mask) * own, own, 2)

    out_parts = [lax.dynamic_slice_in_dim(out_weight, (z ^ mask) * own, own, 1) for mask in range(seq)]
    out_turned = jnp.concatenate(out_parts, axis=1)
    taps = lax.dynamic_slice_in_dim(short_taps, z * own, own, 2)
    whole = whole.transpose(1, 0, 2).reshape(sub, model).astype(jnp.float32)
    mean_sq = jnp.mean(whole * whole, axis=1, keepdims=True)
    normed = (whole * lax.rsqrt(mean_sq + EPSILON) * norm_gain).astype(jnp.bfloat16)
    normed = exchange(normed.reshape(sub, seq, depth).transpose(1, 0, 2), "seq")
    parts = spread(normed.reshape(seq * sub, depth), "tensor")
    groups = (tuple(slots[:2]), tuple(slots[2:]))
    terms = []
    aligned = own % 128 == 0 and length <= BLOCK and sub % 16 == 0
    for group in groups:
        pieces = [parts[slot] for slot in group]
        if seq == 4 and aligned:
            terms.append(relay_sum(pieces, in_weight))
        else:
            terms.append(sum_over_seq(jnp.concatenate(pieces), in_part))
    half = tensor // 2
    if aligned:
        lower_gated, upper_gated = local_stage(groups, terms, taps, long_filter, t, seq, sub)
    else:
        gated = plain_stage(terms, taps, long_filter, t, seq, sub)
        lower_gated = jnp.concatenate(gated[:half])
        upper_gated = jnp.concatenate(gated[half:])

    lower = [1 << bit for bit in range(half.bit_length() - 1)]
    held = None
    for chosen, piece in ((slots[half:], upper_gated), (slots[:half], lower_gated)):
        got = [piece] + [hop(piece, "seq", mask) for mask in range(1, seq)]
        got = jnp.concatenate(got, axis=1)
        terms = {}
        for place, slot in enumerate(chosen):
            terms[slot] = jnp.einsum(
                "rc,nc->rn",
                got[place * seq * sub : (place + 1) * seq * sub],
                out_turned,
                preferred_element_type=jnp.float32,
            )
        terms = fold(terms, "tensor", lower)
        if held is None:
            held = hop(terms[half].astype(jnp.bfloat16), "tensor", half)
        else:
            held = (terms[0] + held.astype(jnp.float32)).astype(jnp.bfloat16)
    back = exchange(held.reshape(seq, sub, depth), "seq")
    back = back.transpose(1, 0, 2).reshape(sub, tensor, width).transpose(1, 0, 2)
    summed = exchange(back, "tensor").reshape(rows, width)
    return residual_in + summed.astype(jnp.float32)


def solution(mesh):
    return jax.shard_map(
        shards,
        mesh=mesh,
        in_specs=(
            P(("groups", "seq"), "tensor"),
            P(),
            P(None, "seq", "tensor"),
            P(None, None, "tensor"),
            P(("tensor", "seq"), None),
            P("seq", "tensor"),
        ),
        out_specs=P(("groups", "seq"), "tensor"),
        check_vma=False,
    )
```

```python
import functools

import jax
import jax.numpy as jnp
import numpy as np
from jax import lax
from jax.experimental import pallas as pl
from jax.experimental.pallas import tpu as pltpu
from jax.sharding import PartitionSpec as P


EPSILON = 1e-05
BLOCK = 512


def pick(stacked, index):
    return lax.dynamic_index_in_dim(stacked, index, 0, keepdims=False)


def hop(value, axis, mask):
    count = lax.axis_size(axis)
    return lax.ppermute(value, axis, [(a, a ^ mask) for a in range(count)])


def exchange(blocks, axis):
    me = lax.axis_index(axis)
    count = lax.axis_size(axis)
    got = [pick(blocks, me)]
    got += [hop(pick(blocks, me ^ mask), axis, mask) for mask in range(1, count)]
    got = jnp.stack(got)
    return jnp.stack([pick(got, me ^ source) for source in range(count)])


def spread(value, axis):
    parts = {0: value}
    mask = lax.axis_size(axis) // 2
    while mask:
        for slot, part in list(parts.items()):
            parts[slot ^ mask] = hop(part, axis, mask)
        mask //= 2
    return parts


def fold(parts, axis, masks):
    parts = dict(parts)
    for mask in masks:
        for slot in sorted(parts, reverse=True):
            if slot & mask:
                came = hop(parts.pop(slot).astype(jnp.bfloat16), axis, mask)
                parts[slot ^ mask] = parts[slot ^ mask] + came.astype(jnp.float32)
    return parts


def sum_over_seq(rows, weight_of):
    count = lax.axis_size("seq")
    narrow = weight_of(0).shape[2] % 128 != 0

    def product(mask):
        form = "rd,sdc->scr" if narrow else "rd,sdc->src"
        return jnp.einsum(form, rows, weight_of(mask), preferred_element_type=jnp.float32)

    low = jnp.bfloat16
    if count != 4:
        sent = {mask: product(mask).astype(low) for mask in range(1, count)}
        came = [hop(sent[mask], "seq", mask) for mask in sent]
    else:
        z = lax.axis_index("seq")
        end = (z == 0) | (z == 3)
        first = hop(product(jnp.where(end, 3, 1)).astype(low), "seq", 1)
        second = product(jnp.where(end, 1, 3)).astype(low)
        middle = lax.ppermute(second, "seq", [(1, 2), (2, 1)])
        near = hop(second, "seq", 1)
        rows, first = lax.optimization_barrier((rows, first))
        relayed = jnp.where(end, 0.0, first.astype(jnp.float32))
        last = hop((product(2) + relayed).astype(low), "seq", 2)
        total = product(0) + jnp.where(end, first, near).astype(jnp.float32) + middle.astype(jnp.float32)
        return [total, last]
    if narrow:
        return [term.transpose(0, 2, 1) for term in [product(0)] + came]
    return [product(0)] + came


def tables(block):
    odd = 2 * np.arange(block)[:, None] + 1
    theta = (odd * np.arange(2 * block)[None, :] % (4 * block)) * (np.pi / (2 * block))
    return np.concatenate([np.cos(theta), np.sin(theta)]).astype(np.float32)


def causal_convolution(signal, taps):
    length, channels = signal.shape
    block = min(length, BLOCK)
    count = length // block
    table = jnp.asarray(tables(block))
    forward = table[:, :block]
    taps_all = jnp.einsum("ft,ckt->kfc", forward, taps.reshape(channels, count, block), precision=lax.Precision.HIGH)
    taps_cos, taps_sin = taps_all[:, :block], taps_all[:, block:]
    both = jnp.stack(
        [
            jnp.einsum("ft,tc->fc", forward, signal[one * block : (one + 1) * block], precision=lax.Precision.HIGH)
            for one in range(count)
        ]
    )
    cos, sin = both[:, :block], both[:, block:]
    outputs = []
    spill = None
    for last in range(count):
        real = imag = 0.0
        for one in range(last + 1):
            other = last - one
            real = real + cos[one] * taps_cos[other] - sin[one] * taps_sin[other]
            imag = imag + cos[one] * taps_sin[other] + sin[one] * taps_cos[other]
        both = jnp.concatenate([real, imag])
        reach = block if last == count - 1 else 2 * block
        back = jnp.einsum("ft,fc->tc", table[:, :reach], both, precision=lax.Precision.HIGH) / block
        here = back[:block]
        outputs.append(here if spill is None else here + spill)
        spill = back[block:]
    return outputs[0] if count == 1 else jnp.concatenate(outputs)


def halves(value):
    high = value.astype(jnp.bfloat16)
    return high, (value - high.astype(jnp.float32)).astype(jnp.bfloat16)


def split_tables(block):
    table = tables(block)[:, :block]
    out = []
    for part in (table, table.T / np.float32(block)):
        high = part.astype(jnp.bfloat16)
        out += [high, (part - high.astype(np.float32)).astype(jnp.bfloat16)]
    return out


def wide_dot(high, low, value, dims):
    dot = functools.partial(lax.dot_general, dimension_numbers=(dims, ((), ())), preferred_element_type=jnp.float32)
    upper, lower = halves(value)
    free = 1 - dims[1][0]
    width = value.shape[free]
    both = dot(high, jnp.concatenate([upper, lower], axis=free))
    return both[:, :width] + both[:, width:] + dot(low, upper)


def filter_kernel(high_ref, low_ref, taps_ref, out_ref):
    out_ref[...] = wide_dot(high_ref[...], low_ref[...], taps_ref[...], ((1,), (1,)))


def local_kernel(groups, each, seq, sub, t_ref, taps_ref, *refs):
    count = each * len(groups)
    moved = count + 5
    sources, outs = refs[:moved], refs[moved : moved + 2]
    proj, gated, sems = refs[moved + 2 : moved + 5]
    held = refs[moved + 5 :]
    copies = [pltpu.make_async_copy(sources[i], held[i], sems.at[i]) for i in range(moved)]
    for copy in copies:
        copy.start()
    terms = held[:count]
    fore_high, fore_low, spectrum_ref, back_high, back_low = held[count:]
    t = t_ref[0]
    length = gated.shape[0]
    shard = length // seq
    tensor = shard // sub

    def place(slot, source, lead):
        return pl.ds(pl.multiple_of(lead + source * shard + (t ^ slot) * sub, 8), sub)

    proj[:, :8] = jnp.zeros((proj.shape[0], 8, proj.shape[2]), jnp.float32)
    for group, slots in enumerate(groups):
        mine = terms[group * each : (group + 1) * each]
        for copy in copies[group * each : (group + 1) * each]:
            copy.wait()
        for position, slot in enumerate(slots):
            for source in range(seq):
                rows = pl.ds((position * seq + source) * sub, sub)
                total = mine[0][:, rows]
                for term in mine[1:]:
                    total = total + term[:, rows].astype(jnp.float32)
                proj[:, place(slot, source, 8)] = total

    def mixed(stream):
        total = taps_ref[stream, 0:1] * proj[stream, pl.ds(8, length)]
        for offset in range(1, taps_ref.shape[1]):
            total = total + taps_ref[stream, offset : offset + 1] * proj[stream, pl.ds(8 - offset, length)]
        return total

    signal = mixed(1) * mixed(2)
    for copy in copies[count : count + 3]:
        copy.wait()
    both = wide_dot(fore_high[...], fore_low[...], signal, ((1,), (0,)))
    cos, sin = both[:length], both[length:]
    taps_cos, taps_sin = spectrum_ref[:length], spectrum_ref[length:]
    both = jnp.concatenate([cos * taps_cos - sin * taps_sin, cos * taps_sin + sin * taps_cos])
    for copy in copies[count + 3 :]:
        copy.wait()
    gated[...] = mixed(0) * wide_dot(back_high[...], back_low[...], both, ((1,), (0,)))
    for slot in range(tensor):
        out = outs[slot // (tensor // 2)]
        for source in range(seq):
            row = ((slot % (tensor // 2)) * seq + source) * sub
            out[row : row + sub] = gated[place(slot, source, 0)].astype(jnp.bfloat16)


def local_stage(groups, terms, taps, long_filter, t, seq, sub):
    own, length = long_filter.shape
    wide = split_tables(length)
    vmem = pl.BlockSpec(memory_space=pltpu.VMEM)
    make_spectrum = pl.pallas_call(
        filter_kernel,
        out_shape=jax.ShapeDtypeStruct((2 * length, own), jnp.float32),
        in_specs=[vmem] * 3,
        out_specs=vmem,
        name="filter_spectrum",
        cost_estimate=pl.CostEstimate(flops=12 * length * length * own, bytes_accessed=4 * length * length, transcendentals=0),
    )
    spectrum = make_spectrum(*wide[:2], long_filter)
    flat = [term for group in terms for term in group]
    lines = length // 2
    moved = [*flat, *wide[:2], spectrum, *wide[2:]]
    return pl.pallas_call(
        functools.partial(local_kernel, groups, len(terms[0]), seq, sub),
        out_shape=[jax.ShapeDtypeStruct((lines, own), jnp.bfloat16)] * 2,
        in_specs=[pl.BlockSpec(memory_space=pltpu.SMEM), vmem] + [pl.BlockSpec(memory_space=pl.ANY)] * len(moved),
        out_specs=[vmem] * 2,
        scratch_shapes=[
            pltpu.VMEM((3, length + 8, own), jnp.float32),
            pltpu.VMEM((length, own), jnp.float32),
            pltpu.SemaphoreType.DMA((len(moved),)),
            *(pltpu.VMEM(part.shape, part.dtype) for part in moved),
        ],
        name="filters",
        cost_estimate=pl.CostEstimate(flops=24 * length * length * own, bytes_accessed=8 * length * length, transcendentals=0),
    )(t.reshape(1).astype(jnp.int32), taps, *moved)


def plain_stage(terms, taps, long_filter, t, seq, sub):
    streams, _, own = terms[0][0].shape
    length = long_filter.shape[1]
    tensor = length // (seq * sub)
    sums = []
    for group in terms:
        total = group[0]
        for term in group[1:]:
            total = total + term.astype(jnp.float32)
        sums.append(total)
    slots = range(tensor)
    projected = jnp.concatenate(sums, axis=1).reshape(streams, tensor, seq, sub, own)
    projected = jnp.stack([lax.dynamic_index_in_dim(projected, t ^ slot, 1, keepdims=False) for slot in slots], axis=2)
    projected = projected.reshape(streams, length, own)
    reach = taps.shape[1] - 1
    padded = jnp.pad(projected, ((0, 0), (reach, 0), (0, 0)))
    mixed = 0.0
    for offset in range(reach + 1):
        mixed = mixed + taps[:, offset, None] * padded[:, reach - offset : reach - offset + length]
    query, key, value = mixed
    conv = causal_convolution(key * value, long_filter)
    gated = (query * conv).astype(jnp.bfloat16).reshape(seq, tensor, sub, own)
    gated = [lax.dynamic_index_in_dim(gated, t ^ slot, 1, keepdims=False) for slot in slots]
    return [rows.reshape(seq * sub, own) for rows in gated]


def shards(residual_in, norm_gain, in_weight, short_taps, long_filter, out_weight):
    seq, tensor = lax.axis_size("seq"), lax.axis_size("tensor")
    z, t = lax.axis_index("seq"), lax.axis_index("tensor")
    rows, width = residual_in.shape
    _, depth, channels = in_weight.shape
    model = width * tensor
    sub = rows // tensor
    own = channels // seq
    length = rows * seq
    slots = range(tensor)

    whole = exchange(residual_in.astype(jnp.bfloat16).reshape(tensor, sub, width), "tensor")

    def in_part(mask):
        return lax.dynamic_slice_in_dim(in_weight, (z ^ mask) * own, own, 2)

    out_parts = [lax.dynamic_slice_in_dim(out_weight, (z ^ mask) * own, own, 1) for mask in range(seq)]
    out_turned = jnp.concatenate(out_parts, axis=1)
    taps = lax.dynamic_slice_in_dim(short_taps, z * own, own, 2)
    whole = whole.transpose(1, 0, 2).reshape(sub, model).astype(jnp.float32)
    mean_sq = jnp.mean(whole * whole, axis=1, keepdims=True)
    normed = (whole * lax.rsqrt(mean_sq + EPSILON) * norm_gain).astype(jnp.bfloat16)
    normed = exchange(normed.reshape(sub, seq, depth).transpose(1, 0, 2), "seq")
    parts = spread(normed.reshape(seq * sub, depth), "tensor")
    groups = (tuple(slots[:2]), tuple(slots[2:]))
    terms = []
    for group in groups:
        rows_of = lax.optimization_barrier(jnp.concatenate([parts[slot] for slot in group]))
        terms.append(sum_over_seq(rows_of, in_part))
    half = tensor // 2
    if own % 128 == 0 and length <= BLOCK and sub % 16 == 0:
        lower_gated, upper_gated = local_stage(groups, terms, taps, long_filter, t, seq, sub)
    else:
        gated = plain_stage(terms, taps, long_filter, t, seq, sub)
        lower_gated = jnp.concatenate(gated[:half])
        upper_gated = jnp.concatenate(gated[half:])

    lower = [1 << bit for bit in range(half.bit_length() - 1)]
    held = None
    for chosen, piece in ((slots[half:], upper_gated), (slots[:half], lower_gated)):
        got = [piece] + [hop(piece, "seq", mask) for mask in range(1, seq)]
        got = jnp.concatenate(got, axis=1)
        terms = {}
        for place, slot in enumerate(chosen):
            terms[slot] = jnp.einsum(
                "rc,nc->rn",
                got[place * seq * sub : (place + 1) * seq * sub],
                out_turned,
                preferred_element_type=jnp.float32,
            )
        terms = fold(terms, "tensor", lower)
        if held is None:
            held = hop(terms[half].astype(jnp.bfloat16), "tensor", half)
        else:
            held = (terms[0] + held.astype(jnp.float32)).astype(jnp.bfloat16)
    back = exchange(held.reshape(seq, sub, depth), "seq")
    back = back.transpose(1, 0, 2).reshape(sub, tensor, width).transpose(1, 0, 2)
    summed = exchange(back, "tensor").reshape(rows, width)
    return residual_in + summed.astype(jnp.float32)


def solution(mesh):
    return jax.shard_map(
        shards,
        mesh=mesh,
        in_specs=(
            P(("groups", "seq"), "tensor"),
            P(),
            P(None, "seq", "tensor"),
            P(None, None, "tensor"),
            P(("tensor", "seq"), None),
            P("seq", "tensor"),
        ),
        out_specs=P(("groups", "seq"), "tensor"),
        check_vma=False,
    )
```

```python
import functools

import jax
import jax.numpy as jnp
import numpy as np
from jax import lax
from jax.experimental import pallas as pl
from jax.experimental.pallas import tpu as pltpu
from jax.sharding import PartitionSpec as P


EPSILON = 1e-05
BLOCK = 512


def pick(stacked, index):
    return lax.dynamic_index_in_dim(stacked, index, 0, keepdims=False)


def hop(value, axis, mask):
    count = lax.axis_size(axis)
    return lax.ppermute(value, axis, [(a, a ^ mask) for a in range(count)])


def exchange(blocks, axis):
    me = lax.axis_index(axis)
    count = lax.axis_size(axis)
    got = [pick(blocks, me)]
    got += [hop(pick(blocks, me ^ mask), axis, mask) for mask in range(1, count)]
    got = jnp.stack(got)
    return jnp.stack([pick(got, me ^ source) for source in range(count)])


def spread(value, axis):
    parts = {0: value}
    mask = lax.axis_size(axis) // 2
    while mask:
        for slot, part in list(parts.items()):
            parts[slot ^ mask] = hop(part, axis, mask)
        mask //= 2
    return parts


def fold(parts, axis, masks):
    parts = dict(parts)
    for mask in masks:
        for slot in sorted(parts, reverse=True):
            if slot & mask:
                came = hop(parts.pop(slot).astype(jnp.bfloat16), axis, mask)
                parts[slot ^ mask] = parts[slot ^ mask] + came.astype(jnp.float32)
    return parts


def sum_over_seq(rows, weight_of):
    count = lax.axis_size("seq")
    narrow = weight_of(0).shape[2] % 128 != 0

    def product(mask):
        form = "rd,sdc->scr" if narrow else "rd,sdc->src"
        return jnp.einsum(form, rows, weight_of(mask), preferred_element_type=jnp.float32)

    low = jnp.bfloat16
    if count != 4:
        sent = {mask: product(mask).astype(low) for mask in range(1, count)}
        came = [hop(sent[mask], "seq", mask) for mask in sent]
    else:
        z = lax.axis_index("seq")
        end = (z == 0) | (z == 3)
        first = hop(product(jnp.where(end, 3, 1)).astype(low), "seq", 1)
        second = product(jnp.where(end, 1, 3)).astype(low)
        middle = lax.ppermute(second, "seq", [(1, 2), (2, 1)])
        near = lax.ppermute(second, "seq", [(0, 1), (3, 2)])
        rows, first = lax.optimization_barrier((rows, first))
        relayed = jnp.where(end, 0.0, first.astype(jnp.float32))
        last = hop((product(2) + relayed).astype(low), "seq", 2)
        total = product(0) + jnp.where(end, first, 0.0).astype(jnp.float32) + middle.astype(jnp.float32)
        return [total, last, near]
    if narrow:
        return [term.transpose(0, 2, 1) for term in [product(0)] + came]
    return [product(0)] + came


def tables(block):
    odd = 2 * np.arange(block)[:, None] + 1
    theta = (odd * np.arange(2 * block)[None, :] % (4 * block)) * (np.pi / (2 * block))
    return np.concatenate([np.cos(theta), np.sin(theta)]).astype(np.float32)


def causal_convolution(signal, taps):
    length, channels = signal.shape
    block = min(length, BLOCK)
    count = length // block
    table = jnp.asarray(tables(block))
    forward = table[:, :block]
    taps_all = jnp.einsum("ft,ckt->kfc", forward, taps.reshape(channels, count, block), precision=lax.Precision.HIGH)
    taps_cos, taps_sin = taps_all[:, :block], taps_all[:, block:]
    both = jnp.stack(
        [
            jnp.einsum("ft,tc->fc", forward, signal[one * block : (one + 1) * block], precision=lax.Precision.HIGH)
            for one in range(count)
        ]
    )
    cos, sin = both[:, :block], both[:, block:]
    outputs = []
    spill = None
    for last in range(count):
        real = imag = 0.0
        for one in range(last + 1):
            other = last - one
            real = real + cos[one] * taps_cos[other] - sin[one] * taps_sin[other]
            imag = imag + cos[one] * taps_sin[other] + sin[one] * taps_cos[other]
        both = jnp.concatenate([real, imag])
        reach = block if last == count - 1 else 2 * block
        back = jnp.einsum("ft,fc->tc", table[:, :reach], both, precision=lax.Precision.HIGH) / block
        here = back[:block]
        outputs.append(here if spill is None else here + spill)
        spill = back[block:]
    return outputs[0] if count == 1 else jnp.concatenate(outputs)


def halves(value):
    high = value.astype(jnp.bfloat16)
    return high, (value - high.astype(jnp.float32)).astype(jnp.bfloat16)


def split_tables(block):
    table = tables(block)[:, :block]
    out = []
    for part in (table, table.T / np.float32(block)):
        high = part.astype(jnp.bfloat16)
        out += [high, (part - high.astype(np.float32)).astype(jnp.bfloat16)]
    return out


def wide_dot(high, low, value, dims):
    dot = functools.partial(lax.dot_general, dimension_numbers=(dims, ((), ())), preferred_element_type=jnp.float32)
    upper, lower = halves(value)
    free = 1 - dims[1][0]
    width = value.shape[free]
    both = dot(high, jnp.concatenate([upper, lower], axis=free))
    return both[:, :width] + both[:, width:] + dot(low, upper)


def filter_kernel(high_ref, low_ref, taps_ref, out_ref):
    out_ref[...] = wide_dot(high_ref[...], low_ref[...], taps_ref[...], ((1,), (1,)))


def local_kernel(groups, each, seq, sub, t_ref, taps_ref, *refs):
    count = each * len(groups)
    moved = count + 5
    sources, outs = refs[:moved], refs[moved : moved + 2]
    proj, gated, sems = refs[moved + 2 : moved + 5]
    held = refs[moved + 5 :]
    copies = [pltpu.make_async_copy(sources[i], held[i], sems.at[i]) for i in range(moved)]
    for copy in copies:
        copy.start()
    terms = held[:count]
    fore_high, fore_low, spectrum_ref, back_high, back_low = held[count:]
    t = t_ref[0]
    length = gated.shape[0]
    shard = length // seq
    tensor = shard // sub

    def place(slot, source, lead):
        return pl.ds(pl.multiple_of(lead + source * shard + (t ^ slot) * sub, 8), sub)

    proj[:, :8] = jnp.zeros((proj.shape[0], 8, proj.shape[2]), jnp.float32)
    for group, slots in enumerate(groups):
        mine = terms[group * each : (group + 1) * each]
        for copy in copies[group * each : (group + 1) * each]:
            copy.wait()
        for position, slot in enumerate(slots):
            for source in range(seq):
                rows = pl.ds((position * seq + source) * sub, sub)
                total = mine[0][:, rows]
                for term in mine[1:]:
                    total = total + term[:, rows].astype(jnp.float32)
                proj[:, place(slot, source, 8)] = total

    def mixed(stream):
        total = taps_ref[stream, 0:1] * proj[stream, pl.ds(8, length)]
        for offset in range(1, taps_ref.shape[1]):
            total = total + taps_ref[stream, offset : offset + 1] * proj[stream, pl.ds(8 - offset, length)]
        return total

    signal = mixed(1) * mixed(2)
    for copy in copies[count : count + 3]:
        copy.wait()
    both = wide_dot(fore_high[...], fore_low[...], signal, ((1,), (0,)))
    cos, sin = both[:length], both[length:]
    taps_cos, taps_sin = spectrum_ref[:length], spectrum_ref[length:]
    both = jnp.concatenate([cos * taps_cos - sin * taps_sin, cos * taps_sin + sin * taps_cos])
    for copy in copies[count + 3 :]:
        copy.wait()
    gated[...] = mixed(0) * wide_dot(back_high[...], back_low[...], both, ((1,), (0,)))
    for slot in range(tensor):
        out = outs[slot // (tensor // 2)]
        for source in range(seq):
            row = ((slot % (tensor // 2)) * seq + source) * sub
            out[row : row + sub] = gated[place(slot, source, 0)].astype(jnp.bfloat16)


def local_stage(groups, terms, taps, long_filter, t, seq, sub):
    own, length = long_filter.shape
    wide = split_tables(length)
    vmem = pl.BlockSpec(memory_space=pltpu.VMEM)
    make_spectrum = pl.pallas_call(
        filter_kernel,
        out_shape=jax.ShapeDtypeStruct((2 * length, own), jnp.float32),
        in_specs=[vmem] * 3,
        out_specs=vmem,
        name="filter_spectrum",
        cost_estimate=pl.CostEstimate(flops=12 * length * length * own, bytes_accessed=4 * length * length, transcendentals=0),
    )
    spectrum = make_spectrum(*wide[:2], long_filter)
    flat = [term for group in terms for term in group]
    lines = length // 2
    moved = [*flat, *wide[:2], spectrum, *wide[2:]]
    return pl.pallas_call(
        functools.partial(local_kernel, groups, len(terms[0]), seq, sub),
        out_shape=[jax.ShapeDtypeStruct((lines, own), jnp.bfloat16)] * 2,
        in_specs=[pl.BlockSpec(memory_space=pltpu.SMEM), vmem] + [pl.BlockSpec(memory_space=pl.ANY)] * len(moved),
        out_specs=[vmem] * 2,
        scratch_shapes=[
            pltpu.VMEM((3, length + 8, own), jnp.float32),
            pltpu.VMEM((length, own), jnp.float32),
            pltpu.SemaphoreType.DMA((len(moved),)),
            *(pltpu.VMEM(part.shape, part.dtype) for part in moved),
        ],
        name="filters",
        cost_estimate=pl.CostEstimate(flops=24 * length * length * own, bytes_accessed=8 * length * length, transcendentals=0),
    )(t.reshape(1).astype(jnp.int32), taps, *moved)


def plain_stage(terms, taps, long_filter, t, seq, sub):
    streams, _, own = terms[0][0].shape
    length = long_filter.shape[1]
    tensor = length // (seq * sub)
    sums = []
    for group in terms:
        total = group[0]
        for term in group[1:]:
            total = total + term.astype(jnp.float32)
        sums.append(total)
    slots = range(tensor)
    projected = jnp.concatenate(sums, axis=1).reshape(streams, tensor, seq, sub, own)
    projected = jnp.stack([lax.dynamic_index_in_dim(projected, t ^ slot, 1, keepdims=False) for slot in slots], axis=2)
    projected = projected.reshape(streams, length, own)
    reach = taps.shape[1] - 1
    padded = jnp.pad(projected, ((0, 0), (reach, 0), (0, 0)))
    mixed = 0.0
    for offset in range(reach + 1):
        mixed = mixed + taps[:, offset, None] * padded[:, reach - offset : reach - offset + length]
    query, key, value = mixed
    conv = causal_convolution(key * value, long_filter)
    gated = (query * conv).astype(jnp.bfloat16).reshape(seq, tensor, sub, own)
    gated = [lax.dynamic_index_in_dim(gated, t ^ slot, 1, keepdims=False) for slot in slots]
    return [rows.reshape(seq * sub, own) for rows in gated]


def shards(residual_in, norm_gain, in_weight, short_taps, long_filter, out_weight):
    seq, tensor = lax.axis_size("seq"), lax.axis_size("tensor")
    z, t = lax.axis_index("seq"), lax.axis_index("tensor")
    rows, width = residual_in.shape
    _, depth, channels = in_weight.shape
    model = width * tensor
    sub = rows // tensor
    own = channels // seq
    length = rows * seq
    slots = range(tensor)

    whole = exchange(residual_in.astype(jnp.bfloat16).reshape(tensor, sub, width), "tensor")

    def in_part(mask):
        return lax.dynamic_slice_in_dim(in_weight, (z ^ mask) * own, own, 2)

    out_parts = [lax.dynamic_slice_in_dim(out_weight, (z ^ mask) * own, own, 1) for mask in range(seq)]
    out_turned = jnp.concatenate(out_parts, axis=1)
    taps = lax.dynamic_slice_in_dim(short_taps, z * own, own, 2)
    whole = whole.transpose(1, 0, 2).reshape(sub, model).astype(jnp.float32)
    mean_sq = jnp.mean(whole * whole, axis=1, keepdims=True)
    normed = (whole * lax.rsqrt(mean_sq + EPSILON) * norm_gain).astype(jnp.bfloat16)
    normed = exchange(normed.reshape(sub, seq, depth).transpose(1, 0, 2), "seq")
    parts = spread(normed.reshape(seq * sub, depth), "tensor")
    groups = (tuple(slots[:2]), tuple(slots[2:]))
    terms = []
    for group in groups:
        rows_of = lax.optimization_barrier(jnp.concatenate([parts[slot] for slot in group]))
        terms.append(sum_over_seq(rows_of, in_part))
    half = tensor // 2
    if own % 128 == 0 and length <= BLOCK and sub % 16 == 0:
        lower_gated, upper_gated = local_stage(groups, terms, taps, long_filter, t, seq, sub)
    else:
        gated = plain_stage(terms, taps, long_filter, t, seq, sub)
        lower_gated = jnp.concatenate(gated[:half])
        upper_gated = jnp.concatenate(gated[half:])

    lower = [1 << bit for bit in range(half.bit_length() - 1)]
    held = None
    for chosen, piece in ((slots[half:], upper_gated), (slots[:half], lower_gated)):
        got = [piece] + [hop(piece, "seq", mask) for mask in range(1, seq)]
        got = jnp.concatenate(got, axis=1)
        terms = {}
        for place, slot in enumerate(chosen):
            terms[slot] = jnp.einsum(
                "rc,nc->rn",
                got[place * seq * sub : (place + 1) * seq * sub],
                out_turned,
                preferred_element_type=jnp.float32,
            )
        terms = fold(terms, "tensor", lower)
        if held is None:
            held = hop(terms[half].astype(jnp.bfloat16), "tensor", half)
        else:
            held = (terms[0] + held.astype(jnp.float32)).astype(jnp.bfloat16)
    back = exchange(held.reshape(seq, sub, depth), "seq")
    back = back.transpose(1, 0, 2).reshape(sub, tensor, width).transpose(1, 0, 2)
    summed = exchange(back, "tensor").reshape(rows, width)
    return residual_in + summed.astype(jnp.float32)


def solution(mesh):
    return jax.shard_map(
        shards,
        mesh=mesh,
        in_specs=(
            P(("groups", "seq"), "tensor"),
            P(),
            P(None, "seq", "tensor"),
            P(None, None, "tensor"),
            P(("tensor", "seq"), None),
            P("seq", "tensor"),
        ),
        out_specs=P(("groups", "seq"), "tensor"),
        check_vma=False,
    )
```

```python
import functools

import jax
import jax.numpy as jnp
import numpy as np
from jax import lax
from jax.experimental import pallas as pl
from jax.experimental.pallas import tpu as pltpu
from jax.sharding import PartitionSpec as P


EPSILON = 1e-05
BLOCK = 512


def pick(stacked, index):
    return lax.dynamic_index_in_dim(stacked, index, 0, keepdims=False)


def hop(value, axis, mask):
    count = lax.axis_size(axis)
    return lax.ppermute(value, axis, [(a, a ^ mask) for a in range(count)])


def exchange(blocks, axis):
    me = lax.axis_index(axis)
    masks = range(1, lax.axis_size(axis))
    came = [hop(pick(blocks, me ^ mask).astype(jnp.bfloat16), axis, mask) for mask in masks]
    own = pick(blocks, me).astype(jnp.bfloat16)
    return arrange(jnp.broadcast_to(own, blocks.shape), came, me)


def arrange(held, came, me):
    for mask, part in enumerate(came, 1):
        held = lax.dynamic_update_index_in_dim(held, part, me ^ mask, 0)
    return held


def spread(value, axis):
    parts = {0: value}
    mask = lax.axis_size(axis) // 2
    while mask:
        for slot, part in list(parts.items()):
            parts[slot ^ mask] = hop(part, axis, mask)
        mask //= 2
    return parts


def fold(parts, axis, masks):
    parts = dict(parts)
    for mask in masks:
        for slot in sorted(parts, reverse=True):
            if slot & mask:
                came = hop(parts.pop(slot).astype(jnp.bfloat16), axis, mask)
                parts[slot ^ mask] = parts[slot ^ mask] + came.astype(jnp.float32)
    return parts


def sum_over_seq(rows, weight_of):
    count = lax.axis_size("seq")
    narrow = weight_of(0).shape[2] % 128 != 0

    def product(mask):
        form = "rd,sdc->scr" if narrow else "rd,sdc->src"
        return jnp.einsum(form, rows, weight_of(mask), preferred_element_type=jnp.float32)

    low = jnp.bfloat16
    if count != 4:
        sent = {mask: product(mask).astype(low) for mask in range(1, count)}
        came = [hop(sent[mask], "seq", mask) for mask in sent]
    else:
        z = lax.axis_index("seq")
        end = (z == 0) | (z == 3)
        first = hop(product(jnp.where(end, 3, 1)).astype(low), "seq", 1)
        second = product(jnp.where(end, 1, 3)).astype(low)
        middle = lax.ppermute(second, "seq", [(1, 2), (2, 1)])
        near = lax.ppermute(second, "seq", [(0, 1), (3, 2)])
        rows, first = lax.optimization_barrier((rows, first))
        relayed = jnp.where(end, 0.0, first.astype(jnp.float32))
        last = hop((product(2) + relayed).astype(low), "seq", 2)
        total = product(0) + jnp.where(end, first, 0.0).astype(jnp.float32) + middle.astype(jnp.float32)
        return [total, last, near]
    if narrow:
        return [term.transpose(0, 2, 1) for term in [product(0)] + came]
    return [product(0)] + came


def tables(block):
    odd = 2 * np.arange(block)[:, None] + 1
    theta = (odd * np.arange(2 * block)[None, :] % (4 * block)) * (np.pi / (2 * block))
    return np.concatenate([np.cos(theta), np.sin(theta)]).astype(np.float32)


def causal_convolution(signal, taps):
    length, channels = signal.shape
    block = min(length, BLOCK)
    count = length // block
    table = jnp.asarray(tables(block))
    forward = table[:, :block]
    taps_all = jnp.einsum("ft,ckt->kfc", forward, taps.reshape(channels, count, block), precision=lax.Precision.HIGH)
    taps_cos, taps_sin = taps_all[:, :block], taps_all[:, block:]
    both = jnp.stack(
        [
            jnp.einsum("ft,tc->fc", forward, signal[one * block : (one + 1) * block], precision=lax.Precision.HIGH)
            for one in range(count)
        ]
    )
    cos, sin = both[:, :block], both[:, block:]
    outputs = []
    spill = None
    for last in range(count):
        real = imag = 0.0
        for one in range(last + 1):
            other = last - one
            real = real + cos[one] * taps_cos[other] - sin[one] * taps_sin[other]
            imag = imag + cos[one] * taps_sin[other] + sin[one] * taps_cos[other]
        both = jnp.concatenate([real, imag])
        reach = block if last == count - 1 else 2 * block
        back = jnp.einsum("ft,fc->tc", table[:, :reach], both, precision=lax.Precision.HIGH) / block
        here = back[:block]
        outputs.append(here if spill is None else here + spill)
        spill = back[block:]
    return outputs[0] if count == 1 else jnp.concatenate(outputs)


def halves(value):
    high = value.astype(jnp.bfloat16)
    return high, (value - high.astype(jnp.float32)).astype(jnp.bfloat16)


def split_tables(block):
    table = tables(block)[:, :block]
    out = []
    for part in (table, table.T / np.float32(block)):
        high = part.astype(jnp.bfloat16)
        out += [high, (part - high.astype(np.float32)).astype(jnp.bfloat16)]
    return out


def wide_dot(high, low, value, dims):
    dot = functools.partial(lax.dot_general, dimension_numbers=(dims, ((), ())), preferred_element_type=jnp.float32)
    upper, lower = halves(value)
    free = 1 - dims[1][0]
    width = value.shape[free]
    both = dot(high, jnp.concatenate([upper, lower], axis=free))
    return both[:, :width] + both[:, width:] + dot(low, upper)


def filter_kernel(high_ref, low_ref, taps_ref, out_ref):
    out_ref[...] = wide_dot(high_ref[...], low_ref[...], taps_ref[...], ((1,), (1,)))


def local_kernel(groups, each, seq, sub, t_ref, *refs):
    count = each * len(groups)
    moved = count + 6
    sources, outs = refs[:moved], refs[moved : moved + 2]
    proj, gated, sems = refs[moved + 2 : moved + 5]
    held = refs[moved + 5 :]
    copies = [pltpu.make_async_copy(sources[i], held[i], sems.at[i]) for i in range(moved)]
    for copy in copies:
        copy.start()
    terms = held[:count]
    fore_high, fore_low, spectrum_ref, back_high, back_low, taps_ref = held[count:]
    t = t_ref[0]
    length = gated.shape[0]
    shard = length // seq
    tensor = shard // sub

    def place(slot, source, lead):
        return pl.ds(pl.multiple_of(lead + source * shard + (t ^ slot) * sub, 8), sub)

    proj[:, :8] = jnp.zeros((proj.shape[0], 8, proj.shape[2]), jnp.float32)
    for group, slots in enumerate(groups):
        mine = terms[group * each : (group + 1) * each]
        for copy in copies[group * each : (group + 1) * each]:
            copy.wait()
        for position, slot in enumerate(slots):
            for source in range(seq):
                rows = pl.ds((position * seq + source) * sub, sub)
                total = mine[0][:, rows]
                for term in mine[1:]:
                    total = total + term[:, rows].astype(jnp.float32)
                proj[:, place(slot, source, 8)] = total

    def mixed(stream):
        total = taps_ref[stream, 0:1] * proj[stream, pl.ds(8, length)]
        for offset in range(1, taps_ref.shape[1]):
            total = total + taps_ref[stream, offset : offset + 1] * proj[stream, pl.ds(8 - offset, length)]
        return total

    copies[count + 5].wait()
    signal = mixed(1) * mixed(2)
    for copy in copies[count : count + 3]:
        copy.wait()
    both = wide_dot(fore_high[...], fore_low[...], signal, ((1,), (0,)))
    cos, sin = both[:length], both[length:]
    taps_cos, taps_sin = spectrum_ref[:length], spectrum_ref[length:]
    both = jnp.concatenate([cos * taps_cos - sin * taps_sin, cos * taps_sin + sin * taps_cos])
    for copy in copies[count + 3 : count + 5]:
        copy.wait()
    gated[...] = mixed(0) * wide_dot(back_high[...], back_low[...], both, ((1,), (0,)))
    for slot in range(tensor):
        out = outs[slot // (tensor // 2)]
        for source in range(seq):
            row = ((slot % (tensor // 2)) * seq + source) * sub
            out[row : row + sub] = gated[place(slot, source, 0)].astype(jnp.bfloat16)


def local_stage(groups, terms, taps, long_filter, t, seq, sub):
    own, length = long_filter.shape
    wide = split_tables(length)
    vmem = pl.BlockSpec(memory_space=pltpu.VMEM)
    make_spectrum = pl.pallas_call(
        filter_kernel,
        out_shape=jax.ShapeDtypeStruct((2 * length, own), jnp.float32),
        in_specs=[vmem] * 3,
        out_specs=vmem,
        name="filter_spectrum",
        cost_estimate=pl.CostEstimate(flops=12 * length * length * own, bytes_accessed=4 * length * length, transcendentals=0),
    )
    spectrum = make_spectrum(*wide[:2], long_filter)
    flat = [term for group in terms for term in group]
    lines = length // 2
    moved = [*flat, *wide[:2], spectrum, *wide[2:], taps]
    return pl.pallas_call(
        functools.partial(local_kernel, groups, len(terms[0]), seq, sub),
        out_shape=[jax.ShapeDtypeStruct((lines, own), jnp.bfloat16)] * 2,
        in_specs=[pl.BlockSpec(memory_space=pltpu.SMEM)] + [pl.BlockSpec(memory_space=pl.ANY)] * len(moved),
        out_specs=[vmem] * 2,
        scratch_shapes=[
            pltpu.VMEM((3, length + 8, own), jnp.float32),
            pltpu.VMEM((length, own), jnp.float32),
            pltpu.SemaphoreType.DMA((len(moved),)),
            *(pltpu.VMEM(part.shape, part.dtype) for part in moved),
        ],
        name="filters",
        cost_estimate=pl.CostEstimate(flops=24 * length * length * own, bytes_accessed=8 * length * length, transcendentals=0),
    )(t.reshape(1).astype(jnp.int32), *moved)


def plain_stage(terms, taps, long_filter, t, seq, sub):
    streams, _, own = terms[0][0].shape
    length = long_filter.shape[1]
    tensor = length // (seq * sub)
    sums = []
    for group in terms:
        total = group[0]
        for term in group[1:]:
            total = total + term.astype(jnp.float32)
        sums.append(total)
    slots = range(tensor)
    projected = jnp.concatenate(sums, axis=1).reshape(streams, tensor, seq, sub, own)
    projected = jnp.stack([lax.dynamic_index_in_dim(projected, t ^ slot, 1, keepdims=False) for slot in slots], axis=2)
    projected = projected.reshape(streams, length, own)
    reach = taps.shape[1] - 1
    padded = jnp.pad(projected, ((0, 0), (reach, 0), (0, 0)))
    mixed = 0.0
    for offset in range(reach + 1):
        mixed = mixed + taps[:, offset, None] * padded[:, reach - offset : reach - offset + length]
    query, key, value = mixed
    conv = causal_convolution(key * value, long_filter)
    gated = (query * conv).astype(jnp.bfloat16).reshape(seq, tensor, sub, own)
    gated = [lax.dynamic_index_in_dim(gated, t ^ slot, 1, keepdims=False) for slot in slots]
    return [rows.reshape(seq * sub, own) for rows in gated]


def shards(residual_in, norm_gain, in_weight, short_taps, long_filter, out_weight):
    seq, tensor = lax.axis_size("seq"), lax.axis_size("tensor")
    z, t = lax.axis_index("seq"), lax.axis_index("tensor")
    rows, width = residual_in.shape
    _, depth, channels = in_weight.shape
    model = width * tensor
    sub = rows // tensor
    own = channels // seq
    length = rows * seq
    slots = range(tensor)

    whole = exchange(residual_in.reshape(tensor, sub, width), "tensor")

    def in_part(mask):
        return lax.dynamic_slice_in_dim(in_weight, (z ^ mask) * own, own, 2)

    out_parts = [lax.dynamic_slice_in_dim(out_weight, (z ^ mask) * own, own, 1) for mask in range(seq)]
    out_turned = jnp.concatenate(out_parts, axis=1)
    taps = lax.dynamic_slice_in_dim(short_taps, z * own, own, 2)
    whole = whole.transpose(1, 0, 2).reshape(sub, model).astype(jnp.float32)
    mean_sq = jnp.mean(whole * whole, axis=1, keepdims=True)
    normed = (whole * lax.rsqrt(mean_sq + EPSILON) * norm_gain).astype(jnp.bfloat16)
    normed = exchange(normed.reshape(sub, seq, depth).transpose(1, 0, 2), "seq")
    parts = spread(normed.reshape(seq * sub, depth), "tensor")
    groups = (tuple(slots[:2]), tuple(slots[2:]))
    terms = []
    for group in groups:
        rows_of = lax.optimization_barrier(jnp.concatenate([parts[slot] for slot in group]))
        terms.append(sum_over_seq(rows_of, in_part))
    half = tensor // 2
    if own % 128 == 0 and length <= BLOCK and sub % 16 == 0:
        lower_gated, upper_gated = local_stage(groups, terms, taps, long_filter, t, seq, sub)
    else:
        gated = plain_stage(terms, taps, long_filter, t, seq, sub)
        lower_gated = jnp.concatenate(gated[:half])
        upper_gated = jnp.concatenate(gated[half:])

    lower = [1 << bit for bit in range(half.bit_length() - 1)]
    totals = []
    for chosen, piece in ((slots[half:], upper_gated), (slots[:half], lower_gated)):
        got = [piece] + [hop(piece, "seq", mask) for mask in range(1, seq)]
        if totals:
            got, totals[0] = lax.optimization_barrier((got, totals[0]))
        got = jnp.concatenate(got, axis=1)
        terms = {}
        for place, slot in enumerate(chosen):
            terms[slot] = jnp.einsum(
                "rc,nc->rn",
                got[place * seq * sub : (place + 1) * seq * sub],
                out_turned,
                preferred_element_type=jnp.float32,
            )
        totals.append(fold(terms, "tensor", lower)[chosen[0]])
    pairs = seq // 2
    side = z // pairs
    crossing = totals[0].astype(jnp.bfloat16).reshape(2, pairs, sub, depth)
    kept = totals[1].reshape(2, pairs, sub, depth)
    sums = []
    for which in (1 - side, side):
        came = hop(pick(crossing, which), "tensor", half)
        if sums:
            kept, sums[0] = lax.optimization_barrier((kept, sums[0]))
        sums.append((pick(kept, which) + came.astype(jnp.float32)).astype(jnp.bfloat16))
    came = []
    for mask in range(1, seq):
        block = pick(sums[0] if mask >= pairs else sums[1], (z ^ mask) % pairs)
        came.append(hop(block, "seq", mask))
    back = arrange(jnp.concatenate([sums[1], sums[1]]), came, z)
    back = back.transpose(1, 0, 2).reshape(sub, tensor, width).transpose(1, 0, 2)
    summed = exchange(back, "tensor").reshape(rows, width)
    return residual_in + summed.astype(jnp.float32)


def solution(mesh):
    return jax.shard_map(
        shards,
        mesh=mesh,
        in_specs=(
            P(("groups", "seq"), "tensor"),
            P(),
            P(None, "seq", "tensor"),
            P(None, None, "tensor"),
            P(("tensor", "seq"), None),
            P("seq", "tensor"),
        ),
        out_specs=P(("groups", "seq"), "tensor"),
        check_vma=False,
    )
```

```python
import functools

import jax
import jax.numpy as jnp
import numpy as np
from jax import lax
from jax.experimental import pallas as pl
from jax.experimental.pallas import tpu as pltpu
from jax.sharding import PartitionSpec as P


EPSILON = 1e-05
BLOCK = 512


def pick(stacked, index):
    return lax.dynamic_index_in_dim(stacked, index, 0, keepdims=False)


def hop(value, axis, mask):
    count = lax.axis_size(axis)
    return lax.ppermute(value, axis, [(a, a ^ mask) for a in range(count)])


def exchange(blocks, axis):
    me = lax.axis_index(axis)
    count = lax.axis_size(axis)
    got = [pick(blocks, me)]
    got += [hop(pick(blocks, me ^ mask), axis, mask) for mask in range(1, count)]
    got = jnp.stack(got)
    return jnp.stack([pick(got, me ^ source) for source in range(count)])


def spread(value, axis):
    parts = {0: value}
    mask = lax.axis_size(axis) // 2
    while mask:
        for slot, part in list(parts.items()):
            parts[slot ^ mask] = hop(part, axis, mask)
        mask //= 2
    return parts


def fold(parts, axis, masks):
    parts = dict(parts)
    for mask in masks:
        for slot in sorted(parts, reverse=True):
            if slot & mask:
                came = hop(parts.pop(slot).astype(jnp.bfloat16), axis, mask)
                parts[slot ^ mask] = parts[slot ^ mask] + came.astype(jnp.float32)
    return parts


def sum_over_seq(rows, weight_of):
    count = lax.axis_size("seq")
    narrow = weight_of(0).shape[2] % 128 != 0

    def product(mask):
        form = "rd,sdc->scr" if narrow else "rd,sdc->src"
        return jnp.einsum(form, rows, weight_of(mask), preferred_element_type=jnp.float32)

    low = jnp.bfloat16
    if count != 4:
        sent = {mask: product(mask).astype(low) for mask in range(1, count)}
        came = [hop(sent[mask], "seq", mask) for mask in sent]
    else:
        z = lax.axis_index("seq")
        end = (z == 0) | (z == 3)
        first = hop(product(jnp.where(end, 3, 1)).astype(low), "seq", 1)
        second = product(jnp.where(end, 1, 3)).astype(low)
        middle = lax.ppermute(second, "seq", [(1, 2), (2, 1)])
        near = lax.ppermute(second, "seq", [(0, 1), (3, 2)])
        rows, first = lax.optimization_barrier((rows, first))
        relayed = jnp.where(end, 0.0, first.astype(jnp.float32))
        last = hop((product(2) + relayed).astype(low), "seq", 2)
        total = product(0) + jnp.where(end, first, 0.0).astype(jnp.float32) + middle.astype(jnp.float32)
        return [total, last, near]
    if narrow:
        return [term.transpose(0, 2, 1) for term in [product(0)] + came]
    return [product(0)] + came


def tables(block):
    odd = 2 * np.arange(block)[:, None] + 1
    theta = (odd * np.arange(2 * block)[None, :] % (4 * block)) * (np.pi / (2 * block))
    return np.concatenate([np.cos(theta), np.sin(theta)]).astype(np.float32)


def causal_convolution(signal, taps):
    length, channels = signal.shape
    block = min(length, BLOCK)
    count = length // block
    table = jnp.asarray(tables(block))
    forward = table[:, :block]
    taps_all = jnp.einsum("ft,ckt->kfc", forward, taps.reshape(channels, count, block), precision=lax.Precision.HIGH)
    taps_cos, taps_sin = taps_all[:, :block], taps_all[:, block:]
    both = jnp.stack(
        [
            jnp.einsum("ft,tc->fc", forward, signal[one * block : (one + 1) * block], precision=lax.Precision.HIGH)
            for one in range(count)
        ]
    )
    cos, sin = both[:, :block], both[:, block:]
    outputs = []
    spill = None
    for last in range(count):
        real = imag = 0.0
        for one in range(last + 1):
            other = last - one
            real = real + cos[one] * taps_cos[other] - sin[one] * taps_sin[other]
            imag = imag + cos[one] * taps_sin[other] + sin[one] * taps_cos[other]
        both = jnp.concatenate([real, imag])
        reach = block if last == count - 1 else 2 * block
        back = jnp.einsum("ft,fc->tc", table[:, :reach], both, precision=lax.Precision.HIGH) / block
        here = back[:block]
        outputs.append(here if spill is None else here + spill)
        spill = back[block:]
    return outputs[0] if count == 1 else jnp.concatenate(outputs)


def halves(value):
    high = value.astype(jnp.bfloat16)
    return high, (value - high.astype(jnp.float32)).astype(jnp.bfloat16)


def split_table(block):
    table = tables(block)[:, :block]
    high = table.astype(jnp.bfloat16)
    return [high, (table - high.astype(np.float32)).astype(jnp.bfloat16)]


def wide_dot(high, low, value, dims):
    dot = functools.partial(lax.dot_general, dimension_numbers=(dims, ((), ())), preferred_element_type=jnp.float32)
    upper, lower = halves(value)
    free = 1 - dims[1][0]
    width = value.shape[free]
    both = dot(high, jnp.concatenate([upper, lower], axis=free))
    return both[:, :width] + both[:, width:] + dot(low, upper)


def filter_kernel(high_ref, low_ref, taps_ref, out_ref):
    out_ref[...] = wide_dot(high_ref[...], low_ref[...], taps_ref[...], ((1,), (1,)))


def local_kernel(groups, each, seq, sub, t_ref, taps_ref, *refs):
    count = each * len(groups)
    moved = count + 3
    sources, outs = refs[:moved], refs[moved : moved + 2]
    proj, gated, sems = refs[moved + 2 : moved + 5]
    held = refs[moved + 5 :]
    copies = [pltpu.make_async_copy(sources[i], held[i], sems.at[i]) for i in range(moved)]
    for copy in copies:
        copy.start()
    terms = held[:count]
    high_ref, low_ref, spectrum_ref = held[count:]
    t = t_ref[0]
    length = gated.shape[0]
    shard = length // seq
    tensor = shard // sub

    def place(slot, source, lead):
        return pl.ds(pl.multiple_of(lead + source * shard + (t ^ slot) * sub, 8), sub)

    proj[:, :8] = jnp.zeros((proj.shape[0], 8, proj.shape[2]), jnp.float32)
    for group, slots in enumerate(groups):
        mine = terms[group * each : (group + 1) * each]
        for copy in copies[group * each : (group + 1) * each]:
            copy.wait()
        for position, slot in enumerate(slots):
            for source in range(seq):
                rows = pl.ds((position * seq + source) * sub, sub)
                total = mine[0][:, rows]
                for term in mine[1:]:
                    total = total + term[:, rows].astype(jnp.float32)
                proj[:, place(slot, source, 8)] = total

    def mixed(stream):
        total = taps_ref[stream, 0:1] * proj[stream, pl.ds(8, length)]
        for offset in range(1, taps_ref.shape[1]):
            total = total + taps_ref[stream, offset : offset + 1] * proj[stream, pl.ds(8 - offset, length)]
        return total

    signal = mixed(1) * mixed(2)
    for copy in copies[count : count + 3]:
        copy.wait()
    both = wide_dot(high_ref[...], low_ref[...], signal, ((1,), (0,)))
    cos, sin = both[:length], both[length:]
    taps_cos, taps_sin = spectrum_ref[:length], spectrum_ref[length:]
    both = jnp.concatenate([cos * taps_cos - sin * taps_sin, cos * taps_sin + sin * taps_cos])
    upper, lower = halves(both.T)
    dot = functools.partial(jnp.dot, preferred_element_type=jnp.float32)
    back = dot(jnp.concatenate([upper, lower]), high_ref[...])
    back = back[: upper.shape[0]] + back[upper.shape[0] :] + dot(upper, low_ref[...])
    gated[...] = mixed(0) * back.T * (1.0 / length)
    for slot in range(tensor):
        out = outs[slot // (tensor // 2)]
        for source in range(seq):
            row = ((slot % (tensor // 2)) * seq + source) * sub
            out[row : row + sub] = gated[place(slot, source, 0)].astype(jnp.bfloat16)


def local_stage(groups, terms, taps, long_filter, t, seq, sub):
    own, length = long_filter.shape
    wide = split_table(length)
    vmem = pl.BlockSpec(memory_space=pltpu.VMEM)
    make_spectrum = pl.pallas_call(
        filter_kernel,
        out_shape=jax.ShapeDtypeStruct((2 * length, own), jnp.float32),
        in_specs=[vmem] * 3,
        out_specs=vmem,
        name="filter_spectrum",
        compiler_params=pltpu.CompilerParams(vmem_limit_bytes=32 * 2**20),
        cost_estimate=pl.CostEstimate(flops=12 * length * length * own, bytes_accessed=4 * length * length, transcendentals=0),
    )
    spectrum = make_spectrum(*wide, long_filter)
    flat = [term for group in terms for term in group]
    lines = length // 2
    moved = [*flat, *wide, spectrum]
    return pl.pallas_call(
        functools.partial(local_kernel, groups, len(terms[0]), seq, sub),
        out_shape=[jax.ShapeDtypeStruct((lines, own), jnp.bfloat16)] * 2,
        in_specs=[pl.BlockSpec(memory_space=pltpu.SMEM), vmem] + [pl.BlockSpec(memory_space=pl.ANY)] * len(moved),
        out_specs=[vmem] * 2,
        scratch_shapes=[
            pltpu.VMEM((3, length + 8, own), jnp.float32),
            pltpu.VMEM((length, own), jnp.float32),
            pltpu.SemaphoreType.DMA((len(moved),)),
            *(pltpu.VMEM(part.shape, part.dtype) for part in moved),
        ],
        name="filters",
        compiler_params=pltpu.CompilerParams(vmem_limit_bytes=32 * 2**20),
        cost_estimate=pl.CostEstimate(flops=24 * length * length * own, bytes_accessed=8 * length * length, transcendentals=0),
    )(t.reshape(1).astype(jnp.int32), taps, *moved)


def plain_stage(terms, taps, long_filter, t, seq, sub):
    streams, _, own = terms[0][0].shape
    length = long_filter.shape[1]
    tensor = length // (seq * sub)
    sums = []
    for group in terms:
        total = group[0]
        for term in group[1:]:
            total = total + term.astype(jnp.float32)
        sums.append(total)
    slots = range(tensor)
    projected = jnp.concatenate(sums, axis=1).reshape(streams, tensor, seq, sub, own)
    projected = jnp.stack([lax.dynamic_index_in_dim(projected, t ^ slot, 1, keepdims=False) for slot in slots], axis=2)
    projected = projected.reshape(streams, length, own)
    reach = taps.shape[1] - 1
    padded = jnp.pad(projected, ((0, 0), (reach, 0), (0, 0)))
    mixed = 0.0
    for offset in range(reach + 1):
        mixed = mixed + taps[:, offset, None] * padded[:, reach - offset : reach - offset + length]
    query, key, value = mixed
    conv = causal_convolution(key * value, long_filter)
    gated = (query * conv).astype(jnp.bfloat16).reshape(seq, tensor, sub, own)
    gated = [lax.dynamic_index_in_dim(gated, t ^ slot, 1, keepdims=False) for slot in slots]
    return [rows.reshape(seq * sub, own) for rows in gated]


def shards(residual_in, norm_gain, in_weight, short_taps, long_filter, out_weight):
    seq, tensor = lax.axis_size("seq"), lax.axis_size("tensor")
    z, t = lax.axis_index("seq"), lax.axis_index("tensor")
    rows, width = residual_in.shape
    _, depth, channels = in_weight.shape
    model = width * tensor
    sub = rows // tensor
    own = channels // seq
    length = rows * seq
    slots = range(tensor)

    whole = exchange(residual_in.astype(jnp.bfloat16).reshape(tensor, sub, width), "tensor")

    def in_part(mask):
        return lax.dynamic_slice_in_dim(in_weight, (z ^ mask) * own, own, 2)

    out_parts = [lax.dynamic_slice_in_dim(out_weight, (z ^ mask) * own, own, 1) for mask in range(seq)]
    out_turned = jnp.concatenate(out_parts, axis=1)
    taps = lax.dynamic_slice_in_dim(short_taps, z * own, own, 2)
    whole = whole.transpose(1, 0, 2).reshape(sub, model).astype(jnp.float32)
    mean_sq = jnp.mean(whole * whole, axis=1, keepdims=True)
    normed = (whole * lax.rsqrt(mean_sq + EPSILON) * norm_gain).astype(jnp.bfloat16)
    normed = exchange(normed.reshape(sub, seq, depth).transpose(1, 0, 2), "seq")
    parts = spread(normed.reshape(seq * sub, depth), "tensor")
    groups = (tuple(slots[:2]), tuple(slots[2:]))
    terms = []
    for group in groups:
        rows_of = lax.optimization_barrier(jnp.concatenate([parts[slot] for slot in group]))
        terms.append(sum_over_seq(rows_of, in_part))
    half = tensor // 2
    if own % 128 == 0 and length <= BLOCK and sub % 16 == 0:
        lower_gated, upper_gated = local_stage(groups, terms, taps, long_filter, t, seq, sub)
    else:
        gated = plain_stage(terms, taps, long_filter, t, seq, sub)
        lower_gated = jnp.concatenate(gated[:half])
        upper_gated = jnp.concatenate(gated[half:])

    lower = [1 << bit for bit in range(half.bit_length() - 1)]
    held = None
    for chosen, piece in ((slots[half:], upper_gated), (slots[:half], lower_gated)):
        got = [piece] + [hop(piece, "seq", mask) for mask in range(1, seq)]
        got = jnp.concatenate(got, axis=1)
        terms = {}
        for place, slot in enumerate(chosen):
            terms[slot] = jnp.einsum(
                "rc,nc->rn",
                got[place * seq * sub : (place + 1) * seq * sub],
                out_turned,
                preferred_element_type=jnp.float32,
            )
        terms = fold(terms, "tensor", lower)
        if held is None:
            held = hop(terms[half].astype(jnp.bfloat16), "tensor", half)
        else:
            held = (terms[0] + held.astype(jnp.float32)).astype(jnp.bfloat16)
    back = exchange(held.reshape(seq, sub, depth), "seq")
    back = back.transpose(1, 0, 2).reshape(sub, tensor, width).transpose(1, 0, 2)
    summed = exchange(back, "tensor").reshape(rows, width)
    return residual_in + summed.astype(jnp.float32)


def solution(mesh):
    return jax.shard_map(
        shards,
        mesh=mesh,
        in_specs=(
            P(("groups", "seq"), "tensor"),
            P(),
            P(None, "seq", "tensor"),
            P(None, None, "tensor"),
            P(("tensor", "seq"), None),
            P("seq", "tensor"),
        ),
        out_specs=P(("groups", "seq"), "tensor"),
        check_vma=False,
    )
```

```python
import functools

import jax
import jax.numpy as jnp
import numpy as np
from jax import lax
from jax.experimental import pallas as pl
from jax.experimental.pallas import tpu as pltpu
from jax.sharding import PartitionSpec as P


EPSILON = 1e-05
BLOCK = 512


def pick(stacked, index):
    return lax.dynamic_index_in_dim(stacked, index, 0, keepdims=False)


def hop(value, axis, mask):
    count = lax.axis_size(axis)
    return lax.ppermute(value, axis, [(a, a ^ mask) for a in range(count)])


def exchange(blocks, axis):
    me = lax.axis_index(axis)
    count = lax.axis_size(axis)
    got = [pick(blocks, me)]
    got += [hop(pick(blocks, me ^ mask), axis, mask) for mask in range(1, count)]
    got = jnp.stack(got)
    return jnp.stack([pick(got, me ^ source) for source in range(count)])


def spread(value, axis):
    parts = {0: value}
    mask = lax.axis_size(axis) // 2
    while mask:
        for slot, part in list(parts.items()):
            parts[slot ^ mask] = hop(part, axis, mask)
        mask //= 2
    return parts


def fold(parts, axis, masks):
    parts = dict(parts)
    for mask in masks:
        for slot in sorted(parts, reverse=True):
            if slot & mask:
                came = hop(parts.pop(slot).astype(jnp.bfloat16), axis, mask)
                parts[slot ^ mask] = parts[slot ^ mask] + came.astype(jnp.float32)
    return parts


def sum_over_seq(rows, weight_of):
    count = lax.axis_size("seq")
    narrow = weight_of(0).shape[2] % 128 != 0

    def product(mask):
        form = "rd,sdc->scr" if narrow else "rd,sdc->src"
        return jnp.einsum(form, rows, weight_of(mask), preferred_element_type=jnp.float32)

    low = jnp.bfloat16
    if count != 4:
        sent = {mask: product(mask).astype(low) for mask in range(1, count)}
        came = [hop(sent[mask], "seq", mask) for mask in sent]
    else:
        z = lax.axis_index("seq")
        end = (z == 0) | (z == 3)
        first = hop(product(jnp.where(end, 3, 1)).astype(low), "seq", 1)
        second = product(jnp.where(end, 1, 3)).astype(low)
        middle = lax.ppermute(second, "seq", [(1, 2), (2, 1)])
        near = lax.ppermute(second, "seq", [(0, 1), (3, 2)])
        rows, first = lax.optimization_barrier((rows, first))
        relayed = jnp.where(end, 0.0, first.astype(jnp.float32))
        last = hop((product(2) + relayed).astype(low), "seq", 2)
        total = product(0) + jnp.where(end, first, 0.0).astype(jnp.float32) + middle.astype(jnp.float32)
        return [total, last, near]
    if narrow:
        return [term.transpose(0, 2, 1) for term in [product(0)] + came]
    return [product(0)] + came


def tables(block):
    odd = 2 * np.arange(block)[:, None] + 1
    theta = (odd * np.arange(2 * block)[None, :] % (4 * block)) * (np.pi / (2 * block))
    return np.concatenate([np.cos(theta), np.sin(theta)]).astype(np.float32)


def causal_convolution(signal, taps):
    length, channels = signal.shape
    block = min(length, BLOCK)
    count = length // block
    table = jnp.asarray(tables(block))
    forward = table[:, :block]
    taps_all = jnp.einsum("ft,ckt->kfc", forward, taps.reshape(channels, count, block), precision=lax.Precision.HIGH)
    taps_cos, taps_sin = taps_all[:, :block], taps_all[:, block:]
    both = jnp.stack(
        [
            jnp.einsum("ft,tc->fc", forward, signal[one * block : (one + 1) * block], precision=lax.Precision.HIGH)
            for one in range(count)
        ]
    )
    cos, sin = both[:, :block], both[:, block:]
    outputs = []
    spill = None
    for last in range(count):
        real = imag = 0.0
        for one in range(last + 1):
            other = last - one
            real = real + cos[one] * taps_cos[other] - sin[one] * taps_sin[other]
            imag = imag + cos[one] * taps_sin[other] + sin[one] * taps_cos[other]
        both = jnp.concatenate([real, imag])
        reach = block if last == count - 1 else 2 * block
        back = jnp.einsum("ft,fc->tc", table[:, :reach], both, precision=lax.Precision.HIGH) / block
        here = back[:block]
        outputs.append(here if spill is None else here + spill)
        spill = back[block:]
    return outputs[0] if count == 1 else jnp.concatenate(outputs)


def halves(value):
    high = value.astype(jnp.bfloat16)
    return high, (value - high.astype(jnp.float32)).astype(jnp.bfloat16)


def split_table(block):
    table = tables(block)[:, :block]
    high = table.astype(jnp.bfloat16)
    return [high, (table - high.astype(np.float32)).astype(jnp.bfloat16)]


def wide_dot(high, low, value, dims):
    dot = functools.partial(lax.dot_general, dimension_numbers=(dims, ((), ())), preferred_element_type=jnp.float32)
    upper, lower = halves(value)
    free = 1 - dims[1][0]
    width = value.shape[free]
    both = dot(high, jnp.concatenate([upper, lower], axis=free))
    return both[:, :width] + both[:, width:] + dot(low, upper)


def filter_kernel(high_ref, low_ref, taps_ref, out_ref):
    out_ref[...] = wide_dot(high_ref[...], low_ref[...], taps_ref[...], ((1,), (1,)))


def local_kernel(groups, each, seq, sub, t_ref, taps_ref, *refs):
    count = sum(each)
    moved = count + 3
    sources, outs = refs[:moved], refs[moved : moved + 2]
    proj, gated, sems = refs[moved + 2 : moved + 5]
    held = refs[moved + 5 :]
    copies = [pltpu.make_async_copy(sources[i], held[i], sems.at[i]) for i in range(moved)]
    for copy in copies:
        copy.start()
    terms = held[:count]
    high_ref, low_ref, spectrum_ref = held[count:]
    t = t_ref[0]
    length = gated.shape[0]
    shard = length // seq
    tensor = shard // sub

    def place(slot, source, lead):
        return pl.ds(pl.multiple_of(lead + source * shard + (t ^ slot) * sub, 8), sub)

    proj[:, :8] = jnp.zeros((proj.shape[0], 8, proj.shape[2]), jnp.float32)
    for group, slots in enumerate(groups):
        start = sum(each[:group])
        mine = terms[start : start + each[group]]
        for copy in copies[start : start + each[group]]:
            copy.wait()
        for position, slot in enumerate(slots):
            for source in range(seq):
                rows = pl.ds((position * seq + source) * sub, sub)
                total = mine[0][:, rows]
                for term in mine[1:]:
                    total = total + term[:, rows].astype(jnp.float32)
                proj[:, place(slot, source, 8)] = total

    def mixed(stream):
        total = taps_ref[stream, 0:1] * proj[stream, pl.ds(8, length)]
        for offset in range(1, taps_ref.shape[1]):
            total = total + taps_ref[stream, offset : offset + 1] * proj[stream, pl.ds(8 - offset, length)]
        return total

    signal = mixed(1) * mixed(2)
    for copy in copies[count : count + 3]:
        copy.wait()
    both = wide_dot(high_ref[...], low_ref[...], signal, ((1,), (0,)))
    cos, sin = both[:length], both[length:]
    taps_cos, taps_sin = spectrum_ref[:length], spectrum_ref[length:]
    both = jnp.concatenate([cos * taps_cos - sin * taps_sin, cos * taps_sin + sin * taps_cos])
    upper, lower = halves(both.T)
    dot = functools.partial(jnp.dot, preferred_element_type=jnp.float32)
    back = dot(jnp.concatenate([upper, lower]), high_ref[...])
    back = back[: upper.shape[0]] + back[upper.shape[0] :] + dot(upper, low_ref[...])
    gated[...] = mixed(0) * back.T * (1.0 / length)
    for slot in range(tensor):
        out = outs[slot // (tensor // 2)]
        for source in range(seq):
            row = ((slot % (tensor // 2)) * seq + source) * sub
            out[row : row + sub] = gated[place(slot, source, 0)].astype(jnp.bfloat16)


def local_stage(groups, terms, taps, long_filter, t, seq, sub):
    own, length = long_filter.shape
    wide = split_table(length)
    vmem = pl.BlockSpec(memory_space=pltpu.VMEM)
    make_spectrum = pl.pallas_call(
        filter_kernel,
        out_shape=jax.ShapeDtypeStruct((2 * length, own), jnp.float32),
        in_specs=[vmem] * 3,
        out_specs=vmem,
        name="filter_spectrum",
        compiler_params=pltpu.CompilerParams(vmem_limit_bytes=32 * 2**20),
        cost_estimate=pl.CostEstimate(flops=12 * length * length * own, bytes_accessed=4 * length * length, transcendentals=0),
    )
    spectrum = make_spectrum(*wide, long_filter)
    flat = [term for group in terms for term in group]
    lines = length // 2
    moved = [*flat, *wide, spectrum]
    return pl.pallas_call(
        functools.partial(local_kernel, groups, [len(group) for group in terms], seq, sub),
        out_shape=[jax.ShapeDtypeStruct((lines, own), jnp.bfloat16)] * 2,
        in_specs=[pl.BlockSpec(memory_space=pltpu.SMEM), vmem] + [pl.BlockSpec(memory_space=pl.ANY)] * len(moved),
        out_specs=[vmem] * 2,
        scratch_shapes=[
            pltpu.VMEM((3, length + 8, own), jnp.float32),
            pltpu.VMEM((length, own), jnp.float32),
            pltpu.SemaphoreType.DMA((len(moved),)),
            *(pltpu.VMEM(part.shape, part.dtype) for part in moved),
        ],
        name="filters",
        compiler_params=pltpu.CompilerParams(vmem_limit_bytes=32 * 2**20),
        cost_estimate=pl.CostEstimate(flops=24 * length * length * own, bytes_accessed=8 * length * length, transcendentals=0),
    )(t.reshape(1).astype(jnp.int32), taps, *moved)


def plain_stage(terms, taps, long_filter, t, seq, sub):
    streams, _, own = terms[0][0].shape
    length = long_filter.shape[1]
    tensor = length // (seq * sub)
    sums = []
    for group in terms:
        total = group[0]
        for term in group[1:]:
            total = total + term.astype(jnp.float32)
        sums.append(total)
    slots = range(tensor)
    projected = jnp.concatenate(sums, axis=1).reshape(streams, tensor, seq, sub, own)
    projected = jnp.stack([lax.dynamic_index_in_dim(projected, t ^ slot, 1, keepdims=False) for slot in slots], axis=2)
    projected = projected.reshape(streams, length, own)
    reach = taps.shape[1] - 1
    padded = jnp.pad(projected, ((0, 0), (reach, 0), (0, 0)))
    mixed = 0.0
    for offset in range(reach + 1):
        mixed = mixed + taps[:, offset, None] * padded[:, reach - offset : reach - offset + length]
    query, key, value = mixed
    conv = causal_convolution(key * value, long_filter)
    gated = (query * conv).astype(jnp.bfloat16).reshape(seq, tensor, sub, own)
    gated = [lax.dynamic_index_in_dim(gated, t ^ slot, 1, keepdims=False) for slot in slots]
    return [rows.reshape(seq * sub, own) for rows in gated]


def shards(residual_in, norm_gain, in_weight, short_taps, long_filter, out_weight):
    seq, tensor = lax.axis_size("seq"), lax.axis_size("tensor")
    z, t = lax.axis_index("seq"), lax.axis_index("tensor")
    rows, width = residual_in.shape
    _, depth, channels = in_weight.shape
    model = width * tensor
    sub = rows // tensor
    own = channels // seq
    length = rows * seq
    slots = range(tensor)

    whole = exchange(residual_in.astype(jnp.bfloat16).reshape(tensor, sub, width), "tensor")

    def in_part(mask):
        return lax.dynamic_slice_in_dim(in_weight, (z ^ mask) * own, own, 2)

    out_parts = [lax.dynamic_slice_in_dim(out_weight, (z ^ mask) * own, own, 1) for mask in (0, *reversed(range(1, seq)))]
    out_turned = lax.optimization_barrier(jnp.concatenate(out_parts, axis=1))
    taps = lax.dynamic_slice_in_dim(short_taps, z * own, own, 2)
    whole = whole.transpose(1, 0, 2).reshape(sub, model).astype(jnp.float32)
    mean_sq = jnp.mean(whole * whole, axis=1, keepdims=True)
    normed = (whole * lax.rsqrt(mean_sq + EPSILON) * norm_gain).astype(jnp.bfloat16)
    normed = exchange(normed.reshape(sub, seq, depth).transpose(1, 0, 2), "seq")
    parts = spread(normed.reshape(seq * sub, depth), "tensor")
    groups = (tuple(slots[:2]), tuple(slots[2:]))
    terms = []
    for group, name in zip(groups, ("sum_early", "sum_late")):
        rows_of = lax.optimization_barrier(jnp.concatenate([parts[slot] for slot in group]))
        terms.append(sum_over_seq(rows_of, in_part))
        if name == "sum_early":
            total = terms[0][0]
            for term in terms[0][1:]:
                total = total + term.astype(jnp.float32)
            terms[0] = [total]
    half = tensor // 2
    if own % 128 == 0 and length <= BLOCK and sub % 16 == 0:
        lower_gated, upper_gated = local_stage(groups, terms, taps, long_filter, t, seq, sub)
    else:
        gated = plain_stage(terms, taps, long_filter, t, seq, sub)
        lower_gated = jnp.concatenate(gated[:half])
        upper_gated = jnp.concatenate(gated[half:])

    lower = [1 << bit for bit in range(half.bit_length() - 1)]
    held = None
    for chosen, piece in ((slots[half:], upper_gated), (slots[:half], lower_gated)):
        got = [piece] + [hop(piece, "seq", mask) for mask in reversed(range(1, seq))]
        got = jnp.concatenate(got, axis=1)
        terms = {}
        for place, slot in enumerate(chosen):
            terms[slot] = jnp.einsum(
                "rc,nc->rn",
                got[place * seq * sub : (place + 1) * seq * sub],
                out_turned,
                preferred_element_type=jnp.float32,
            )
        terms = fold(terms, "tensor", lower)
        if held is None:
            held = hop(terms[half].astype(jnp.bfloat16), "tensor", half)
        else:
            held = (terms[0] + held.astype(jnp.float32)).astype(jnp.bfloat16)
    back = exchange(held.reshape(seq, sub, depth), "seq")
    back = back.transpose(1, 0, 2).reshape(sub, tensor, width).transpose(1, 0, 2)
    summed = exchange(back, "tensor").reshape(rows, width)
    return residual_in + summed.astype(jnp.float32)


def solution(mesh):
    return jax.shard_map(
        shards,
        mesh=mesh,
        in_specs=(
            P(("groups", "seq"), "tensor"),
            P(),
            P(None, "seq", "tensor"),
            P(None, None, "tensor"),
            P(("tensor", "seq"), None),
            P("seq", "tensor"),
        ),
        out_specs=P(("groups", "seq"), "tensor"),
        check_vma=False,
    )
```
